32 devices in a mesh: gx: 4 (over y, x), gy: 8 (over z, core).
Axes of the slice: x: 2, y: 2, z: 4, core: 2. Of those that a mesh axis runs over, the one named last changes fastest.
Arguments:
- populations: float32 [19, 2, 32, 1024], P(None, None, 'gx', 'gy'), may hold values from 0.3 to 2.3, as said below
- labels: int32 [2, 32, 1024], P(None, 'gx', 'gy'), may hold values 0 or 1
- solid: int32 [2, 32, 1024], P(None, 'gx', 'gy'), may hold values 0 or 1
- rates: float32 [15], replicated, may hold values from 0.7 to 1.8
Outputs:
- final_state: float32 [2, 19, 2, 32, 1024], P(None, None, None, 'gx', 'gy')
The draws below stay inside these ranges and needn't reach their ends.
Inputs may be any that keep to these rules, and one draw needn't show every extreme that they name: `populations`: each value is a population divided by its lattice weight, near equilibrium with a velocity of at most 0.05 a component and a density between 0.7 and 1.3, with a relative roughness of up to 0.3 a population.
All inputs are finite; a program needn't handle non-finite values. No bound on the sum of `labels` or of `solid` on one device may be relied on, other than what follows from the above.
Results may differ from the reference program's by a relative error of at most 0.0001.
Values sent between devices are 32-bit elements; how exact they have to be, the bound alone decides.
No kernel may reach another device: no remote copies, remote signals or barrier semaphores. Data moves between devices by JAX's collectives and lax.ppermute only.
A program may use at most 64 MiB of HBM per device.

```python
import jax
import jax.numpy as jnp
import numpy as np
from jax import lax

DEPTH = 2
ITERS = 6
NX = 32
NY = 1024


velocity_table = np.array([[0, 0, 0], [1, 0, 0], [-1, 0, 0], [0, 1, 0], [0, -1, 0], [0, 0, 1], [0, 0, -1], [1, 1, 0], [-1, -1, 0], [1, -1, 0], [-1, 1, 0], [1, 0, 1], [-1, 0, -1], [1, 0, -1], [-1, 0, 1], [0, 1, 1], [0, -1, -1], [0, 1, -1], [0, -1, 1]])


def draw_populations(key, part):
    subkeys = jax.random.split(jax.random.fold_in(key, 17), 3)
    cell_shape = (DEPTH, NX, NY)
    density = jax.random.uniform(subkeys[0], cell_shape, jnp.float32, 0.7, 1.3)
    roughness = jax.random.uniform(subkeys[2], (19,) + cell_shape, jnp.float32, -0.3, 0.3)
    velocity_field = jax.random.uniform(subkeys[1], (3,) + cell_shape, jnp.float32, -0.05, 0.05)
    velocity = jnp.asarray(velocity_table, jnp.float32)
    projected = jnp.einsum('qd,dxyz->qxyz', velocity, velocity_field)
    squared_speed = jnp.sum(velocity_field * velocity_field, axis=0)
    balance = density[None] * (1.0 + 3.0 * projected + 4.5 * projected * projected - 1.5 * squared_speed[None])
    return (balance * (1.0 + roughness)).astype(jnp.float32)


def set_ends(values, rng, low, largest):
    spot = [jax.random.randint(jax.random.fold_in(rng, axis), (), 0, length) for axis, length in enumerate(values.shape)]
    widest = values.shape.index(max(values.shape))
    next_to = spot[:widest] + [(spot[widest] + 1) % values.shape[widest]] + spot[widest + 1:]
    return values.at[tuple(spot)].set(low).at[tuple(next_to)].set(largest)


def setup_inputs(seed: int = 0) -> dict:
    key_of = jax.random.split(jax.random.key(seed), 5)
    return {
        "populations": draw_populations(jax.random.fold_in(key_of[4], 71), 0),
        "labels": set_ends((jax.random.randint(key_of[1], (DEPTH, NX, NY), 0, 2) < 1).astype(jnp.int32), jax.random.fold_in(key_of[1], 1), 0, 1),
        "solid": set_ends((jax.random.randint(key_of[2], (DEPTH, NX, NY), 0, 4) < 1).astype(jnp.int32), jax.random.fold_in(key_of[2], 1), 0, 1),
        "rates": jnp.clip(jax.random.uniform(key_of[3], (15,), jnp.float32, 0.7, 1.8), 0.7, 1.8),
    }


velocity_table = np.array([[0, 0, 0], [1, 0, 0], [-1, 0, 0], [0, 1, 0], [0, -1, 0], [0, 0, 1], [0, 0, -1], [1, 1, 0], [-1, -1, 0], [1, -1, 0], [-1, 1, 0], [1, 0, 1], [-1, 0, -1], [1, 0, -1], [-1, 0, 1], [0, 1, 1], [0, -1, -1], [0, 1, -1], [0, -1, 1]])
weight_table = np.array([1.0 / 3.0] + [1.0 / 18.0] * 6 + [1.0 / 36.0] * 12)
tension = 0.1
recolor_beta = 0.7
gradient_floor = 0.1

def opposite_of(member):
    return int(np.argmax(np.all(velocity_table == -velocity_table[member], axis=1)))

def build_moments():
    float_table = velocity_table * 1.0
    first_axis = float_table[:, 0]
    second_axis = float_table[:, 1]
    depth_axis = float_table[:, 2]
    squared = first_axis ** 2 + second_axis ** 2 + depth_axis ** 2
    higher = 3.0 * squared - 5.0
    cubic = 5.0 * squared - 9.0
    first_diag = 3.0 * first_axis ** 2 - squared
    cross_diag = second_axis ** 2 - depth_axis ** 2
    listed = [squared * 0.0 + 1.0, 19.0 * squared - 30.0, (21.0 * squared ** 2 - 53.0 * squared + 24.0) / 2.0, first_axis, cubic * first_axis, second_axis, cubic * second_axis, depth_axis, cubic * depth_axis, first_diag, higher * first_diag, cross_diag, higher * cross_diag, first_axis * second_axis, second_axis * depth_axis, first_axis * depth_axis, cross_diag * first_axis, (depth_axis ** 2 - first_axis ** 2) * second_axis, (first_axis ** 2 - second_axis ** 2) * depth_axis]
    return np.array(listed)

def build_placement():
    free_rows = [1, 2, 4, 6, 8] + list(range(9, 19))
    return np.eye(19)[free_rows]

def build_signs():
    return np.array([-1.0] + [1.0] * 18)

def build_lengths():
    return np.maximum(np.sqrt(np.sum((velocity_table * 1.0) ** 2, axis=1)), 1.0)

def lattice_tables():
    velocity = jnp.asarray(velocity_table, jnp.float32)
    weights = jnp.asarray(weight_table, jnp.float32)
    return (velocity, weights)

def relax_matrix(rates):
    moment_table = build_moments()
    inverse_table = moment_table.T / np.sum(moment_table ** 2, axis=1)[None, :]
    relaxation = jnp.dot(rates, jnp.asarray(build_placement(), jnp.float32), precision=lax.Precision.HIGHEST)
    inverse = jnp.asarray(inverse_table, jnp.float32)
    moment = jnp.asarray(moment_table, jnp.float32)
    matrix = jnp.dot(inverse * relaxation[None, :], moment, precision=lax.Precision.HIGHEST)
    weights = jnp.asarray(weight_table, jnp.float32)
    return matrix * weights[None, :] / weights[:, None]

def macroscopic(flattened):
    velocity, weights = lattice_tables()
    moment_rows = jnp.concatenate([weights[None, :], (velocity * weights[:, None]).T], axis=0)
    moments = jnp.dot(moment_rows, flattened[0], precision=lax.Precision.HIGHEST)
    red_mass = jnp.dot(weights[None, :], flattened[1], precision=lax.Precision.HIGHEST)
    return (moments, red_mass)

def collide(flattened, moments, red_mass, gradient, scaled):
    velocity, weights = lattice_tables()
    density = moments[0:1]
    velocity_field = moments[1:4] / density
    projected = jnp.dot(velocity, velocity_field, precision=lax.Precision.HIGHEST)
    squared_speed = lax.optimization_barrier(jnp.sum(velocity_field * velocity_field, axis=0, keepdims=True))
    balance = density * (1.0 + 3.0 * projected + 4.5 * projected * projected - 1.5 * squared_speed)
    relaxed = flattened[0] - jnp.dot(scaled, flattened[0] - balance, precision=lax.Precision.HIGHEST)
    magnitude = jnp.sqrt(lax.optimization_barrier(jnp.sum(gradient * gradient, axis=0, keepdims=True)))
    bounded = jnp.maximum(magnitude, gradient_floor)
    aligned = jnp.dot(velocity, gradient, precision=lax.Precision.HIGHEST)
    sign_column = jnp.asarray(build_signs(), jnp.float32)[:, None]
    relaxed = relaxed + 0.5 * tension * (aligned * aligned / bounded - sign_column * magnitude)
    lengths = jnp.asarray(build_lengths(), jnp.float32)[:, None]
    fraction = red_mass / density
    mixing = recolor_beta * red_mass * (density - red_mass) / density
    recolored = fraction * relaxed + mixing * aligned / (lengths * bounded)
    return jnp.stack([relaxed, recolored])

def gradient_whole(phase_field):
    components = [jnp.zeros(phase_field.shape, jnp.float32) for axis_number in range(3)]
    for member in range(1, 19):
        along_first, along_second, along_depth = (int(value) for value in velocity_table[member])
        shifted = jnp.roll(phase_field, (-along_depth, -along_first, -along_second), axis=(0, 1, 2))
        factor = 3.0 * float(weight_table[member])
        for axis_number, along in enumerate((along_first, along_second, along_depth)):
            if along != 0:
                components[axis_number] = components[axis_number] + factor * along * shifted
    return jnp.stack(components)

def stream_whole(collided, current, blocked):
    results = []
    for member in range(19):
        along_first, along_second, along_depth = (int(value) for value in velocity_table[member])
        shifted = jnp.roll(collided[:, member], (along_depth, along_first, along_second), axis=(1, 2, 3))
        source_rock = jnp.roll(blocked, (along_depth, along_first, along_second), axis=(0, 1, 2))
        bounced = collided[:, opposite_of(member)]
        pulled = jnp.where(source_rock[None], bounced, shifted)
        results.append(jnp.where(blocked[None], current[:, member], pulled))
    return jnp.stack(results, axis=1)

def reference(populations, labels, solid, rates):
    scaled = relax_matrix(rates)
    red_part = labels.astype(jnp.float32)[None] * populations
    current = jnp.stack([populations, red_part])
    blocked = solid > 0
    grid_shape = current.shape
    for iteration in range(ITERS):
        flattened = current.reshape(2, 19, -1)
        moments, red_mass = macroscopic(flattened)
        phase_field = ((2.0 * red_mass - moments[0:1]) / moments[0:1]).reshape(grid_shape[2:])
        gradient = gradient_whole(phase_field).reshape(3, -1)
        collided = collide(flattened, moments, red_mass, gradient, scaled).reshape(grid_shape)
        current = stream_whole(collided, current, blocked)
    return current
```

```python
import jax
import jax.numpy as jnp
import numpy as np
from jax import lax
from jax.experimental import pallas as pl
from jax.experimental.pallas import tpu as pltpu
from jax.sharding import PartitionSpec as P

ITERS = 6


velocity_table = np.array(
    [
        [0, 0, 0],
        [1, 0, 0],
        [-1, 0, 0],
        [0, 1, 0],
        [0, -1, 0],
        [0, 0, 1],
        [0, 0, -1],
        [1, 1, 0],
        [-1, -1, 0],
        [1, -1, 0],
        [-1, 1, 0],
        [1, 0, 1],
        [-1, 0, -1],
        [1, 0, -1],
        [-1, 0, 1],
        [0, 1, 1],
        [0, -1, -1],
        [0, 1, -1],
        [0, -1, 1],
    ]
)
weight_table = np.array([1.0 / 3.0] + [1.0 / 18.0] * 6 + [1.0 / 36.0] * 12)
tension = 0.1
recolor_beta = 0.7
gradient_floor = 0.1


def padded_2(cells, sides, width):
    for axis, dim in sides:
        count = lax.axis_size(axis)
        head = lax.slice_in_dim(cells, 0, width, axis=dim)
        tail = lax.slice_in_dim(cells, cells.shape[dim] - width, cells.shape[dim], axis=dim)
        cells = jnp.concatenate(
            [
                lax.ppermute(tail, axis, [(i, (i + 1) % count) for i in range(count)]),
                cells,
                lax.ppermute(head, axis, [((i + 1) % count, i) for i in range(count)]),
            ],
            axis=dim,
        )
    return cells


def opposite_of(member):
    return int(np.argmax(np.all(velocity_table == -velocity_table[member], axis=1)))


def build_moments():
    float_table = velocity_table * 1.0
    first_axis = float_table[:, 0]
    second_axis = float_table[:, 1]
    depth_axis = float_table[:, 2]
    squared = first_axis**2 + second_axis**2 + depth_axis**2
    higher = 3.0 * squared - 5.0
    cubic = 5.0 * squared - 9.0
    first_diag = 3.0 * first_axis**2 - squared
    cross_diag = second_axis**2 - depth_axis**2
    listed = [
        squared * 0.0 + 1.0,
        19.0 * squared - 30.0,
        (21.0 * squared**2 - 53.0 * squared + 24.0) / 2.0,
        first_axis,
        cubic * first_axis,
        second_axis,
        cubic * second_axis,
        depth_axis,
        cubic * depth_axis,
        first_diag,
        higher * first_diag,
        cross_diag,
        higher * cross_diag,
        first_axis * second_axis,
        second_axis * depth_axis,
        first_axis * depth_axis,
        cross_diag * first_axis,
        (depth_axis**2 - first_axis**2) * second_axis,
        (first_axis**2 - second_axis**2) * depth_axis,
    ]
    return np.array(listed)


def build_placement():
    free_rows = [1, 2, 4, 6, 8] + list(range(9, 19))
    return np.eye(19)[free_rows]


def build_signs():
    return np.array([-1.0] + [1.0] * 18)


def build_lengths():
    return np.maximum(np.sqrt(np.sum((velocity_table * 1.0) ** 2, axis=1)), 1.0)


def lattice_tables():
    velocity = jnp.asarray(velocity_table, jnp.float32)
    weights = jnp.asarray(weight_table, jnp.float32)
    return (velocity, weights)


def relax_matrix(rates):
    moment_table = build_moments()
    inverse_table = moment_table.T / np.sum(moment_table**2, axis=1)[None, :]
    relaxation = jnp.dot(
        rates, jnp.asarray(build_placement(), jnp.float32), precision=lax.Precision.HIGHEST
    )
    inverse = jnp.asarray(inverse_table, jnp.float32)
    moment = jnp.asarray(moment_table, jnp.float32)
    matrix = jnp.dot(inverse * relaxation[None, :], moment, precision=lax.Precision.HIGHEST)
    weights = jnp.asarray(weight_table, jnp.float32)
    return matrix * weights[None, :] / weights[:, None]


def macroscopic(flattened):
    velocity, weights = lattice_tables()
    moment_rows = jnp.concatenate([weights[None, :], (velocity * weights[:, None]).T], axis=0)
    moments = jnp.dot(moment_rows, flattened[0], precision=lax.Precision.HIGHEST)
    red_mass = jnp.dot(weights[None, :], flattened[1], precision=lax.Precision.HIGHEST)
    return (moments, red_mass)


def collide(flattened, moments, red_mass, gradient, scaled):
    velocity, weights = lattice_tables()
    density = moments[0:1]
    velocity_field = moments[1:4] / density
    projected = jnp.dot(velocity, velocity_field, precision=lax.Precision.HIGHEST)
    squared_speed = jnp.sum(velocity_field * velocity_field, axis=0, keepdims=True)
    balance = density * (1.0 + 3.0 * projected + 4.5 * projected * projected - 1.5 * squared_speed)
    relaxed = flattened[0] - jnp.dot(
        scaled, flattened[0] - balance, precision=lax.Precision.HIGHEST
    )
    magnitude = jnp.sqrt(jnp.sum(gradient * gradient, axis=0, keepdims=True))
    bounded = jnp.maximum(magnitude, gradient_floor)
    aligned = jnp.dot(velocity, gradient, precision=lax.Precision.HIGHEST)
    sign_column = jnp.asarray(build_signs(), jnp.float32)[:, None]
    relaxed = relaxed + 0.5 * tension * (aligned * aligned / bounded - sign_column * magnitude)
    lengths = jnp.asarray(build_lengths(), jnp.float32)[:, None]
    fraction = red_mass / density
    mixing = recolor_beta * red_mass * (density - red_mass) / density
    recolored = fraction * relaxed + mixing * aligned / (lengths * bounded)
    return jnp.stack([relaxed, recolored])


def gradient_local(padded_phase, height, breadth):
    components = [
        jnp.zeros((padded_phase.shape[0], height, breadth), jnp.float32) for axis_number in range(3)
    ]
    for member in range(1, 19):
        along_first, along_second, along_depth = (int(value) for value in velocity_table[member])
        window = padded_phase[
            :,
            1 + along_first : 1 + along_first + height,
            1 + along_second : 1 + along_second + breadth,
        ]
        shifted = jnp.roll(window, -along_depth, axis=0)
        factor = 3.0 * float(weight_table[member])
        for axis_number, along in enumerate((along_first, along_second, along_depth)):
            if along != 0:
                components[axis_number] = components[axis_number] + factor * along * shifted
    return jnp.stack(components)


def stream_local(padded, collided, current, solid_pad, blocked, height, breadth):
    results = []
    for member in range(19):
        along_first, along_second, along_depth = (int(value) for value in velocity_table[member])
        window = padded[
            :,
            member,
            :,
            1 - along_first : 1 - along_first + height,
            1 - along_second : 1 - along_second + breadth,
        ]
        shifted = jnp.roll(window, along_depth, axis=1)
        rock_window = solid_pad[
            :,
            1 - along_first : 1 - along_first + height,
            1 - along_second : 1 - along_second + breadth,
        ]
        source_rock = jnp.roll(rock_window, along_depth, axis=0)
        bounced = collided[:, opposite_of(member)]
        pulled = jnp.where(source_rock[None], bounced, shifted)
        results.append(jnp.where(blocked[None], current[:, member], pulled))
    return jnp.stack(results, axis=1)


def body_plain(populations, labels, solid, rates):
    scaled = relax_matrix(rates)
    red_part = labels.astype(jnp.float32)[None] * populations
    current = jnp.stack([populations, red_part])
    height = populations.shape[2]
    breadth = populations.shape[3]
    blocked = solid > 0
    grid_shape = current.shape
    solid_pad = padded_2(solid, (("gx", 1), ("gy", 2)), 1) > 0
    for iteration in range(ITERS):
        flattened = current.reshape(2, 19, -1)
        moments, red_mass = macroscopic(flattened)
        phase_field = ((2.0 * red_mass - moments[0:1]) / moments[0:1]).reshape(grid_shape[2:])
        padded_phase = padded_2(phase_field, (("gx", 1), ("gy", 2)), 1)
        gradient = gradient_local(padded_phase, height, breadth).reshape(3, -1)
        collided = collide(flattened, moments, red_mass, gradient, scaled).reshape(grid_shape)
        padded = padded_2(collided, (("gx", 3), ("gy", 4)), 1)
        current = stream_local(padded, collided, current, solid_pad, blocked, height, breadth)
    return current


SUB = 8
LANES = 128
HALF = LANES // 2
SLOT = 16
REACH = 2 * ITERS
PAIRS = [(m, opposite_of(m)) for m in range(1, 19) if m < opposite_of(m)]


def lane_ids(shape):
    return lax.broadcasted_iota(jnp.int32, shape, len(shape) - 1)


def slot_mask(shape, slots):
    ids = lane_ids(shape) // SLOT
    mask = ids == slots[0]
    for slot in slots[1:]:
        mask = mask | (ids == slot)
    return mask


def lane_roll(value, amount):
    return pltpu.roll(value, amount % LANES, axis=value.ndim - 1)


def moved(planes, swap, along):
    first, second, side = planes
    if swap:
        first, second = second, first
    amount = (HALF if swap else 0) + along
    if amount:
        first, second, side = (lane_roll(p, amount) for p in (first, second, side))
    if along:
        ids = lane_ids(first.shape)
        edge = 0 if along > 0 else LANES - 1
        at_first = ids == edge
        at_second = ids == (edge + HALF) % LANES
        first, second, side = (
            jnp.where(at_first, side, first),
            jnp.where(at_second, side, second),
            jnp.where(at_first, first, jnp.where(at_second, second, side)),
        )
    return first, second, side


def edges_kernel(pop_ref, lab_ref, sol_ref, left_ref, right_ref):
    ids = lane_ids((SUB, LANES))
    low = ids < HALF
    keep_left = slot_mask((SUB, LANES), (0, 4))
    keep_right = slot_mask((SUB, LANES), (7, 3))

    def plane(member):
        if member < 19:
            shallow, deep = pop_ref[member, 0], pop_ref[member, 1]
        elif member == 19:
            shallow, deep = lab_ref[0].astype(jnp.float32), lab_ref[1].astype(jnp.float32)
        else:
            shallow, deep = sol_ref[0].astype(jnp.float32), sol_ref[1].astype(jnp.float32)
        deep = lane_roll(deep, HALF)
        return jnp.where(low, shallow, deep), jnp.where(low, deep, shallow)

    for index in range(11):
        left, right = plane(2 * index)
        if 2 * index + 1 < 21:
            left_next, right_next = plane(2 * index + 1)
            left = jnp.where(keep_left, left, lane_roll(left_next, SLOT))
            right = jnp.where(keep_right, right, lane_roll(right_next, -SLOT))
        left_ref[index] = left
        right_ref[index] = right


def weighted_sum(values):
    axis = values[1]
    for q in range(2, 7):
        axis = axis + values[q]
    diag = values[7]
    for q in range(8, 19):
        diag = diag + values[q]
    return 12.0 * values[0] + 2.0 * axis + diag


def steps_kernel(*refs, tiles):
    pops = refs[: len(tiles)]
    sides = refs[len(tiles) : 2 * len(tiles)]
    rates_ref, out_ref, state, after, phase, total, inverse, red, mask, rock = refs[2 * len(tiles) :]
    norms = np.sum(build_moments() ** 2, axis=1)
    free = [1, 2, 4, 6, 8] + list(range(9, 19))
    rate = {row: rates_ref[k] * float(1.0 / norms[row]) for k, row in enumerate(free)}
    back = slot_mask((SUB, LANES), (0, 4))

    def put_macro(j, rows, density, reds, where=None):
        inv = 1.0 / density
        values = ((total, density), (inverse, inv), (red, reds), (phase, (2.0 * reds - density) * inv))
        for ref, value in values:
            if where is None:
                ref[j, rows, :] = value
            else:
                pltpu.store(ref.at[j, rows, :], value, mask=where)

    for spot, source in enumerate(tiles):
        rows = pl.ds(spot * SUB, SUB)
        pop_ref, side_ref = pops[source], sides[source]

        def side_plane(member):
            packed = side_ref[member // 2]
            if member % 2 == 0:
                return packed
            return jnp.where(back, lane_roll(packed, -SLOT), lane_roll(packed, SLOT))

        labels = (side_ref[11], lane_roll(side_ref[12], HALF), side_plane(19))
        rocks = (side_ref[13], lane_roll(side_ref[14], HALF), side_plane(20))
        sums = [[], [], []]
        for member in range(19):
            values = (
                pop_ref[member, 0],
                lane_roll(pop_ref[member, 1], HALF),
                side_plane(member),
            )
            for j in range(3):
                state[member, j, rows, :] = values[j]
                state[19 + member, j, rows, :] = labels[j] * values[j]
                sums[j].append(values[j])
        for j in range(3):
            rock[j, rows, :] = rocks[j]
            density = weighted_sum(sums[j])
            put_macro(j, rows, density, labels[j] * density)

    def rows_loop(start, count, run):
        tile_count = -(-count // SUB)

        def step(index, carry):
            run(start + index * SUB)
            return carry

        if tile_count == 1:
            run(start)
        else:
            lax.fori_loop(0, tile_count, step, 0)

    first_row = SUB * (len(tiles) // 2)

    def make_masks(base):
        for member in range(1, 19):
            a, b, c = (int(v) for v in velocity_table[member])
            planes = moved([rock[j, pl.ds(base - a, SUB), :] for j in range(3)], c % 2 == 1, b)
            for j in range(3):
                mask[member - 1, j, pl.ds(base, SUB), :] = planes[j]

    rows_loop(first_row - REACH + 2, SUB + 2 * REACH - 4, make_masks)

    axis_a9 = rate[9] + 4.0 * rate[10]
    cross_9 = rate[9] - 2.0 * rate[10]
    diag_9 = rate[9] + rate[10]
    axis_a11 = rate[11] + 4.0 * rate[12]
    cross_11 = rate[11] - 2.0 * rate[12]
    diag_11 = rate[11] + rate[12]

    def gradient_planes(base):
        before = [phase[j, pl.ds(base - 1, SUB), :] for j in range(3)]
        here = [phase[j, pl.ds(base, SUB), :] for j in range(3)]
        behind = [phase[j, pl.ds(base + 1, SUB), :] for j in range(3)]
        slope = [p - m for p, m in zip(behind, before)]
        both = [p + m for p, m in zip(behind, before)]
        rim = [2.0 * h + s for h, s in zip(here, both)]
        slope_up, slope_down = moved(slope, False, -1), moved(slope, False, 1)
        slope_deep = moved(slope, True, 0)
        here_up, here_down = moved(here, False, -1), moved(here, False, 1)
        here_deep = moved(here, True, 0)
        rim_y = [r + (d + d) for r, d in zip(rim, here_deep)]
        rim_up, rim_down = moved(rim_y, False, -1), moved(rim_y, False, 1)
        rim_z = [r + (u + d) for r, u, d in zip(rim, here_up, here_down)]
        deeper, shallower = moved(rim_z, True, 0), moved(rim_z, True, 0)
        scale = 1.0 / 12.0
        return [
            (
                scale * (2.0 * slope[j] + (slope_up[j] + slope_down[j]) + (slope_deep[j] + slope_deep[j])),
                scale * (rim_up[j] - rim_down[j]),
                scale * (deeper[j] - shallower[j]),
            )
            for j in range(3)
        ]

    def collide_plane(j, base, grads):
        rows = pl.ds(base, SUB)
        gx, gy, gz = grads
        density, inv, reds = total[j, rows, :], inverse[j, rows, :], red[j, rows, :]
        value = [state[q, j, rows, :] for q in range(19)]
        even = {p: value[p] + value[o] for p, o in PAIRS}
        odd = {p: value[p] - value[o] for p, o in PAIRS}
        ex, ey, ez = 2.0 * even[1], 2.0 * even[3], 2.0 * even[5]
        ox, oy, oz = 2.0 * odd[1], 2.0 * odd[3], 2.0 * odd[5]
        pxy, pxz, pyz = even[7] + even[9], even[11] + even[13], even[15] + even[17]
        rxy, rxz, ryz = even[7] - even[9], even[11] - even[13], even[15] - even[17]
        x_xy, y_xy = odd[7] + odd[9], odd[7] - odd[9]
        x_xz, z_xz = odd[11] + odd[13], odd[11] - odd[13]
        y_yz, z_yz = odd[15] + odd[17], odd[15] - odd[17]
        tx, ty, tz = x_xy + x_xz, y_xy + y_yz, z_xz + z_yz
        jx, jy, jz = ox + tx, oy + ty, oz + tz
        ux, uy, uz = jx * inv, jy * inv, jz * inv
        xx, yy, zz = jx * ux, jy * uy, jz * uz
        square = xx + yy + zz
        sum_axis = ex + ey + ez
        sum_diag = pxy + pxz + pyz
        rest = 12.0 * value[0]
        d_energy = 8.0 * sum_diag - 11.0 * sum_axis - 30.0 * rest + 11.0 * density - 19.0 * square
        d_second = sum_diag - 4.0 * sum_axis + 12.0 * rest - 3.0 * density + 5.5 * square
        flat_x = 1.5 * xx - 0.5 * square
        flat_w = 0.5 * (yy - zz)
        a9 = 3.0 * ex - sum_axis - flat_x
        b9 = sum_diag - 3.0 * pyz - flat_x
        a11 = ey - ez - flat_w
        b11 = pxy - pxz - flat_w
        axis_x = (0.5 * axis_a9) * a9 + (0.5 * cross_9) * b9
        diag_x = cross_9 * a9 + diag_9 * b9
        axis_w = (0.5 * axis_a11) * a11 + (0.5 * cross_11) * b11
        diag_w = cross_11 * a11 + diag_11 * b11
        norm2 = gx * gx + gy * gy + gz * gz
        size = jnp.sqrt(norm2)
        inv_bound = 1.0 / jnp.maximum(size, gradient_floor)
        pull = (0.5 * tension) * size
        push = (0.5 * tension) * inv_bound
        iso_axis = (-5.5 * rate[1]) * d_energy - (2.0 * rate[2]) * d_second + pull
        iso_diag = (8.0 * rate[1]) * d_energy + rate[2] * d_second + pull
        iso_rest = (-2.5 * rate[1]) * d_energy + rate[2] * d_second - pull
        out_even = {
            1: iso_axis + 2.0 * axis_x,
            3: iso_axis - axis_x + axis_w,
            5: iso_axis - axis_x - axis_w,
        }
        dxy = iso_diag + diag_x + diag_w
        dxz = iso_diag + diag_x - diag_w
        dyz = iso_diag - 2.0 * diag_x
        sxy = rate[13] * (rxy - jx * uy)
        syz = rate[14] * (ryz - jy * uz)
        sxz = rate[15] * (rxz - jx * uz)
        out_even.update(
            {7: dxy + sxy, 9: dxy - sxy, 11: dxz + sxz, 13: dxz - sxz, 15: dyz + syz, 17: dyz - syz}
        )
        third = 2.0 / 3.0
        qx = rate[4] * (tx - 4.0 * ox + third * jx)
        qy = rate[6] * (ty - 4.0 * oy + third * jy)
        qz = rate[8] * (tz - 4.0 * oz + third * jz)
        mx = rate[16] * (x_xy - x_xz)
        my = rate[17] * (y_yz - y_xy)
        mz = rate[18] * (z_xz - z_yz)
        fx, fy = qx + mx, qy - my
        hx, hz = qx - mx, qz + mz
        ky, kz = qy + my, qz - mz
        out_odd = {
            1: -2.0 * qx,
            3: -2.0 * qy,
            5: -2.0 * qz,
            7: fx + fy,
            9: fx - fy,
            11: hx + hz,
            13: hx - hz,
            15: ky + kz,
            17: ky - kz,
        }
        along = {
            1: gx,
            3: gy,
            5: gz,
            7: gx + gy,
            9: gx - gy,
            11: gx + gz,
            13: gx - gz,
            15: gy + gz,
            17: gy - gz,
        }
        fraction = reds * inv
        mixing = (recolor_beta / 36.0) * reds * (1.0 - fraction)
        mix_axis = mixing * inv_bound
        mix_diag = mix_axis * float(1.0 / np.sqrt(2.0))
        relaxed = value[0] - iso_rest
        after[0, j, rows, :] = relaxed
        after[19, j, rows, :] = fraction * relaxed
        for p, o in PAIRS:
            steady = out_even[p] - (along[p] * along[p]) * push
            mixed = along[p] * (mix_axis if p < 7 else mix_diag)
            forth = value[p] - (steady + out_odd[p])
            reverse = value[o] - (steady - out_odd[p])
            after[p, j, rows, :] = forth
            after[o, j, rows, :] = reverse
            after[19 + p, j, rows, :] = fraction * forth + mixed
            after[19 + o, j, rows, :] = fraction * reverse - mixed

    def collide_rows(base):
        grads = gradient_planes(base)
        for j in range(3):
            collide_plane(j, base, grads[j])

    def stream_rows(base):
        rows = pl.ds(base, SUB)
        fluid = [rock[j, rows, :] < 0.5 for j in range(3)]
        sums = [[[], [], []], [[], [], []]]
        for q in range(19):
            a, b, c = (int(v) for v in velocity_table[q])
            back_rows = pl.ds(base - a, SUB)
            if q > 0:
                hits = [mask[q - 1, j, rows, :] > 0.5 for j in range(3)]
            for s in range(2):
                planes = [after[19 * s + q, j, back_rows, :] for j in range(3)]
                if q > 0:
                    planes = moved(planes, c % 2 == 1, b)
                    other = 19 * s + opposite_of(q)
                    planes = [
                        jnp.where(hits[j], after[other, j, rows, :], planes[j]) for j in range(3)
                    ]
                for j in range(3):
                    pltpu.store(state.at[19 * s + q, j, rows, :], planes[j], mask=fluid[j])
                    sums[s][j].append(planes[j])
        for j in range(3):
            put_macro(j, rows, weighted_sum(sums[0][j]), weighted_sum(sums[1][j]), fluid[j])

    for iteration in range(ITERS):
        width = REACH - 2 * iteration
        rows_loop(first_row - width + 1, SUB + 2 * width - 2, collide_rows)
        rows_loop(first_row - width + 2, SUB + 2 * width - 4, stream_rows)

    own = pl.ds(first_row, SUB)
    for s in range(2):
        for q in range(19):
            out_ref[s, q, 0] = state[19 * s + q, 0, own, :]
            out_ref[s, q, 1] = lane_roll(state[19 * s + q, 1, own, :], HALF)


def shifted(value, axis, amount):
    count = lax.axis_size(axis)
    return lax.ppermute(value, axis, [(i, (i + amount) % count) for i in range(count)])


def body_deep(populations, labels, solid, rates):
    count = lax.axis_size("gx")
    amounts = sorted({amount % count for amount in (2, 1, -1, -2)})
    pops = {amount: shifted(populations, "gx", amount) for amount in amounts}
    side_shape = jax.ShapeDtypeStruct((11, SUB, LANES), jnp.float32)
    left, right = pl.pallas_call(edges_kernel, out_shape=(side_shape, side_shape))(
        populations, labels, solid
    )
    from_right = shifted(left, "gy", -1)
    from_left = shifted(right, "gy", 1)
    merged = jnp.where(slot_mask((11, SUB, LANES), (0, 1, 4, 5)), from_right, from_left)
    side = jnp.concatenate([merged, labels.astype(jnp.float32), solid.astype(jnp.float32)], axis=0)
    sides = {amount: shifted(side, "gx", amount) for amount in amounts}
    pops[0], sides[0] = populations, side
    order = sorted(pops)
    tiles = tuple(order.index(amount % count) for amount in (2, 1, 0, -1, -2))
    blocks = len(tiles)
    rows = blocks * SUB
    args = [pops[amount] for amount in order] + [sides[amount] for amount in order]

    def kernel(*refs):
        pop_refs, side_refs = refs[: len(order)], refs[len(order) : 2 * len(order)]
        picked = [pop_refs[k] for k in tiles] + [side_refs[k] for k in tiles]
        steps_kernel(*picked, *refs[2 * len(order) :], tiles=tuple(range(blocks)))

    plane = pltpu.VMEM((3, rows, LANES), jnp.float32)
    vmem = pl.BlockSpec(memory_space=pltpu.VMEM)
    return pl.pallas_call(
        kernel,
        out_shape=jax.ShapeDtypeStruct((2,) + populations.shape, jnp.float32),
        in_specs=[vmem] * len(args) + [pl.BlockSpec(memory_space=pltpu.SMEM)],
        out_specs=vmem,
        scratch_shapes=[
            pltpu.VMEM((38, 3, rows, LANES), jnp.float32),
            pltpu.VMEM((38, 3, rows, LANES), jnp.float32),
            plane,
            plane,
            plane,
            plane,
            pltpu.VMEM((18, 3, rows, LANES), jnp.float32),
            plane,
        ],
    )(*args, rates)


def body(populations, labels, solid, rates):
    depth, height, breadth = populations.shape[1:]
    fits = (depth, height, breadth) == (2, SUB, LANES) and lax.axis_size("gx") >= 4
    if fits and REACH < min(2 * SUB, SLOT):
        return body_deep(populations, labels, solid, rates)
    return body_plain(populations, labels, solid, rates)


def solution(mesh):
    return jax.shard_map(
        body,
        mesh=mesh,
        in_specs=(P(None, None, "gx", "gy"), P(None, "gx", "gy"), P(None, "gx", "gy"), P()),
        out_specs=P(None, None, None, "gx", "gy"),
        check_vma=False,
    )
```

```python
import jax
import jax.numpy as jnp
import numpy as np
from jax import lax
from jax.experimental import pallas as pl
from jax.experimental.pallas import tpu as pltpu
from jax.sharding import PartitionSpec as P

ITERS = 6


velocity_table = np.array(
    [
        [0, 0, 0],
        [1, 0, 0],
        [-1, 0, 0],
        [0, 1, 0],
        [0, -1, 0],
        [0, 0, 1],
        [0, 0, -1],
        [1, 1, 0],
        [-1, -1, 0],
        [1, -1, 0],
        [-1, 1, 0],
        [1, 0, 1],
        [-1, 0, -1],
        [1, 0, -1],
        [-1, 0, 1],
        [0, 1, 1],
        [0, -1, -1],
        [0, 1, -1],
        [0, -1, 1],
    ]
)
weight_table = np.array([1.0 / 3.0] + [1.0 / 18.0] * 6 + [1.0 / 36.0] * 12)
tension = 0.1
recolor_beta = 0.7
gradient_floor = 0.1


def padded_2(cells, sides, width):
    for axis, dim in sides:
        count = lax.axis_size(axis)
        head = lax.slice_in_dim(cells, 0, width, axis=dim)
        tail = lax.slice_in_dim(cells, cells.shape[dim] - width, cells.shape[dim], axis=dim)
        cells = jnp.concatenate(
            [
                lax.ppermute(tail, axis, [(i, (i + 1) % count) for i in range(count)]),
                cells,
                lax.ppermute(head, axis, [((i + 1) % count, i) for i in range(count)]),
            ],
            axis=dim,
        )
    return cells


def opposite_of(member):
    return int(np.argmax(np.all(velocity_table == -velocity_table[member], axis=1)))


def build_moments():
    float_table = velocity_table * 1.0
    first_axis = float_table[:, 0]
    second_axis = float_table[:, 1]
    depth_axis = float_table[:, 2]
    squared = first_axis**2 + second_axis**2 + depth_axis**2
    higher = 3.0 * squared - 5.0
    cubic = 5.0 * squared - 9.0
    first_diag = 3.0 * first_axis**2 - squared
    cross_diag = second_axis**2 - depth_axis**2
    listed = [
        squared * 0.0 + 1.0,
        19.0 * squared - 30.0,
        (21.0 * squared**2 - 53.0 * squared + 24.0) / 2.0,
        first_axis,
        cubic * first_axis,
        second_axis,
        cubic * second_axis,
        depth_axis,
        cubic * depth_axis,
        first_diag,
        higher * first_diag,
        cross_diag,
        higher * cross_diag,
        first_axis * second_axis,
        second_axis * depth_axis,
        first_axis * depth_axis,
        cross_diag * first_axis,
        (depth_axis**2 - first_axis**2) * second_axis,
        (first_axis**2 - second_axis**2) * depth_axis,
    ]
    return np.array(listed)


def build_placement():
    free_rows = [1, 2, 4, 6, 8] + list(range(9, 19))
    return np.eye(19)[free_rows]


def build_signs():
    return np.array([-1.0] + [1.0] * 18)


def build_lengths():
    return np.maximum(np.sqrt(np.sum((velocity_table * 1.0) ** 2, axis=1)), 1.0)


def lattice_tables():
    velocity = jnp.asarray(velocity_table, jnp.float32)
    weights = jnp.asarray(weight_table, jnp.float32)
    return (velocity, weights)


def relax_matrix(rates):
    moment_table = build_moments()
    inverse_table = moment_table.T / np.sum(moment_table**2, axis=1)[None, :]
    relaxation = jnp.dot(
        rates, jnp.asarray(build_placement(), jnp.float32), precision=lax.Precision.HIGHEST
    )
    inverse = jnp.asarray(inverse_table, jnp.float32)
    moment = jnp.asarray(moment_table, jnp.float32)
    matrix = jnp.dot(inverse * relaxation[None, :], moment, precision=lax.Precision.HIGHEST)
    weights = jnp.asarray(weight_table, jnp.float32)
    return matrix * weights[None, :] / weights[:, None]


def macroscopic(flattened):
    velocity, weights = lattice_tables()
    moment_rows = jnp.concatenate([weights[None, :], (velocity * weights[:, None]).T], axis=0)
    moments = jnp.dot(moment_rows, flattened[0], precision=lax.Precision.HIGHEST)
    red_mass = jnp.dot(weights[None, :], flattened[1], precision=lax.Precision.HIGHEST)
    return (moments, red_mass)


def collide(flattened, moments, red_mass, gradient, scaled):
    velocity, weights = lattice_tables()
    density = moments[0:1]
    velocity_field = moments[1:4] / density
    projected = jnp.dot(velocity, velocity_field, precision=lax.Precision.HIGHEST)
    squared_speed = jnp.sum(velocity_field * velocity_field, axis=0, keepdims=True)
    balance = density * (1.0 + 3.0 * projected + 4.5 * projected * projected - 1.5 * squared_speed)
    relaxed = flattened[0] - jnp.dot(
        scaled, flattened[0] - balance, precision=lax.Precision.HIGHEST
    )
    magnitude = jnp.sqrt(jnp.sum(gradient * gradient, axis=0, keepdims=True))
    bounded = jnp.maximum(magnitude, gradient_floor)
    aligned = jnp.dot(velocity, gradient, precision=lax.Precision.HIGHEST)
    sign_column = jnp.asarray(build_signs(), jnp.float32)[:, None]
    relaxed = relaxed + 0.5 * tension * (aligned * aligned / bounded - sign_column * magnitude)
    lengths = jnp.asarray(build_lengths(), jnp.float32)[:, None]
    fraction = red_mass / density
    mixing = recolor_beta * red_mass * (density - red_mass) / density
    recolored = fraction * relaxed + mixing * aligned / (lengths * bounded)
    return jnp.stack([relaxed, recolored])


def gradient_local(padded_phase, height, breadth):
    components = [
        jnp.zeros((padded_phase.shape[0], height, breadth), jnp.float32) for axis_number in range(3)
    ]
    for member in range(1, 19):
        along_first, along_second, along_depth = (int(value) for value in velocity_table[member])
        window = padded_phase[
            :,
            1 + along_first : 1 + along_first + height,
            1 + along_second : 1 + along_second + breadth,
        ]
        shifted = jnp.roll(window, -along_depth, axis=0)
        factor = 3.0 * float(weight_table[member])
        for axis_number, along in enumerate((along_first, along_second, along_depth)):
            if along != 0:
                components[axis_number] = components[axis_number] + factor * along * shifted
    return jnp.stack(components)


def stream_local(padded, collided, current, solid_pad, blocked, height, breadth):
    results = []
    for member in range(19):
        along_first, along_second, along_depth = (int(value) for value in velocity_table[member])
        window = padded[
            :,
            member,
            :,
            1 - along_first : 1 - along_first + height,
            1 - along_second : 1 - along_second + breadth,
        ]
        shifted = jnp.roll(window, along_depth, axis=1)
        rock_window = solid_pad[
            :,
            1 - along_first : 1 - along_first + height,
            1 - along_second : 1 - along_second + breadth,
        ]
        source_rock = jnp.roll(rock_window, along_depth, axis=0)
        bounced = collided[:, opposite_of(member)]
        pulled = jnp.where(source_rock[None], bounced, shifted)
        results.append(jnp.where(blocked[None], current[:, member], pulled))
    return jnp.stack(results, axis=1)


def body_plain(populations, labels, solid, rates):
    scaled = relax_matrix(rates)
    red_part = labels.astype(jnp.float32)[None] * populations
    current = jnp.stack([populations, red_part])
    height = populations.shape[2]
    breadth = populations.shape[3]
    blocked = solid > 0
    grid_shape = current.shape
    solid_pad = padded_2(solid, (("gx", 1), ("gy", 2)), 1) > 0
    for iteration in range(ITERS):
        flattened = current.reshape(2, 19, -1)
        moments, red_mass = macroscopic(flattened)
        phase_field = ((2.0 * red_mass - moments[0:1]) / moments[0:1]).reshape(grid_shape[2:])
        padded_phase = padded_2(phase_field, (("gx", 1), ("gy", 2)), 1)
        gradient = gradient_local(padded_phase, height, breadth).reshape(3, -1)
        collided = collide(flattened, moments, red_mass, gradient, scaled).reshape(grid_shape)
        padded = padded_2(collided, (("gx", 3), ("gy", 4)), 1)
        current = stream_local(padded, collided, current, solid_pad, blocked, height, breadth)
    return current


SUB = 8
LANES = 128
HALF = LANES // 2
SLOT = 16
REACH = 2 * ITERS
PAIRS = [(m, opposite_of(m)) for m in range(1, 19) if m < opposite_of(m)]


def lane_ids(shape):
    return lax.broadcasted_iota(jnp.int32, shape, len(shape) - 1)


def slot_mask(shape, slots):
    ids = lane_ids(shape) // SLOT
    mask = ids == slots[0]
    for slot in slots[1:]:
        mask = mask | (ids == slot)
    return mask


def lane_roll(value, amount):
    return pltpu.roll(value, amount % LANES, axis=value.ndim - 1)


def moved(planes, swap, along):
    first, second, side = planes
    if swap:
        first, second = second, first
    amount = (HALF if swap else 0) + along
    if amount:
        first, second, side = (lane_roll(p, amount) for p in (first, second, side))
    if along:
        ids = lane_ids(first.shape)
        edge = 0 if along > 0 else LANES - 1
        at_first = ids == edge
        at_second = ids == (edge + HALF) % LANES
        first, second, side = (
            jnp.where(at_first, side, first),
            jnp.where(at_second, side, second),
            jnp.where(at_first, first, jnp.where(at_second, second, side)),
        )
    return first, second, side


GROUP = 4
SIDE_COUNT = -(-21 // GROUP)


def edges_kernel(mains, inner_ref, outer_ref):
    even = lax.axis_index("gy") % 2 == 0
    low = lane_ids((SUB, LANES)) < HALF
    spots = [slot_mask((SUB, LANES), (k, 4 + k)) for k in range(GROUP)]
    for spot, main in enumerate(mains):
        for index in range(SIDE_COUNT):
            for k in range(min(GROUP, 21 - GROUP * index)):
                shallow, deep = main[2 * (GROUP * index + k)], main[2 * (GROUP * index + k) + 1]
                deep = lane_roll(deep, HALF)
                left = lane_roll(jnp.where(low, shallow, deep), SLOT * k)
                right = lane_roll(jnp.where(low, deep, shallow), -SLOT * k)
                if k == 0:
                    left_all, right_all = left, right
                else:
                    left_all = jnp.where(spots[k], left, left_all)
                    right_all = jnp.where(spots[GROUP - 1 - k], right, right_all)
            inner_ref[spot * SIDE_COUNT + index] = jnp.where(even, right_all, left_all)
            outer_ref[spot * SIDE_COUNT + index] = jnp.where(even, left_all, right_all)


def weighted_sum(values):
    axis = values[1]
    for q in range(2, 7):
        axis = axis + values[q]
    diag = values[7]
    for q in range(8, 19):
        diag = diag + values[q]
    return 12.0 * values[0] + 2.0 * axis + diag


def steps_kernel(mains, inner_ref, outer_ref, rates_ref, out_ref, *scratch):
    state, after, phase, total, inverse, red, mask, rock = scratch
    gx_index = lax.axis_index("gx")
    even = lax.axis_index("gy") % 2 == 0
    norms = np.sum(build_moments() ** 2, axis=1)
    free = [1, 2, 4, 6, 8] + list(range(9, 19))
    rate = {row: rates_ref[k] * float(1.0 / norms[row]) for k, row in enumerate(free)}
    from_left = slot_mask((SUB, LANES), (0, 4))

    def put_macro(j, rows, density, reds, where=None):
        inv = 1.0 / density
        values = ((total, density), (inverse, inv), (red, reds), (phase, (2.0 * reds - density) * inv))
        for ref, value in values:
            if where is None:
                ref[j, rows, :] = value
            else:
                pltpu.store(ref.at[j, rows, :], value, mask=where)

    for source, (main, spots) in enumerate(zip(mains, tile_spots(gx_index, len(mains)))):
        packs = []
        for index in range(SIDE_COUNT):
            inner = inner_ref[source * SIDE_COUNT + index]
            outer = outer_ref[source * SIDE_COUNT + index]
            packs.append((jnp.where(even, inner, outer), jnp.where(even, outer, inner)))

        def planes_of(member):
            k = member % GROUP
            ahead = lane_roll(packs[member // GROUP][0], -SLOT * k)
            behind = lane_roll(packs[member // GROUP][1], SLOT * k)
            side = jnp.where(from_left, ahead, behind)
            return main[2 * member], lane_roll(main[2 * member + 1], HALF), side

        labels = planes_of(19)
        rocks = planes_of(20)
        sums = [[], [], []]
        places = [pl.ds(pl.multiple_of(spot * SUB, SUB), SUB) for spot in spots]
        for member in range(19):
            values = planes_of(member)
            for j in range(3):
                for rows in places:
                    state[member, j, rows, :] = values[j]
                    state[19 + member, j, rows, :] = labels[j] * values[j]
                sums[j].append(values[j])
        for j in range(3):
            density = weighted_sum(sums[j])
            for rows in places:
                rock[j, rows, :] = rocks[j]
                put_macro(j, rows, density, labels[j] * density)

    def rows_loop(start, count, run):
        tile_count = -(-count // SUB)

        def step(index, carry):
            run(start + index * SUB)
            return carry

        if tile_count == 1:
            run(start)
        else:
            lax.fori_loop(0, tile_count, step, 0)

    first_row = 2 * SUB

    def make_masks(base):
        for member in range(1, 19):
            a, b, c = (int(v) for v in velocity_table[member])
            planes = moved([rock[j, pl.ds(base - a, SUB), :] for j in range(3)], c % 2 == 1, b)
            for j in range(3):
                mask[member - 1, j, pl.ds(base, SUB), :] = planes[j]

    rows_loop(first_row - REACH + 2, SUB + 2 * REACH - 4, make_masks)

    axis_a9 = rate[9] + 4.0 * rate[10]
    cross_9 = rate[9] - 2.0 * rate[10]
    diag_9 = rate[9] + rate[10]
    axis_a11 = rate[11] + 4.0 * rate[12]
    cross_11 = rate[11] - 2.0 * rate[12]
    diag_11 = rate[11] + rate[12]

    def gradient_planes(base):
        before = [phase[j, pl.ds(base - 1, SUB), :] for j in range(3)]
        here = [phase[j, pl.ds(base, SUB), :] for j in range(3)]
        behind = [phase[j, pl.ds(base + 1, SUB), :] for j in range(3)]
        slope = [p - m for p, m in zip(behind, before)]
        both = [p + m for p, m in zip(behind, before)]
        rim = [2.0 * h + s for h, s in zip(here, both)]
        slope_up, slope_down = moved(slope, False, -1), moved(slope, False, 1)
        slope_deep = moved(slope, True, 0)
        here_up, here_down = moved(here, False, -1), moved(here, False, 1)
        here_deep = moved(here, True, 0)
        rim_y = [r + (d + d) for r, d in zip(rim, here_deep)]
        rim_up, rim_down = moved(rim_y, False, -1), moved(rim_y, False, 1)
        rim_z = [r + (u + d) for r, u, d in zip(rim, here_up, here_down)]
        deeper, shallower = moved(rim_z, True, 0), moved(rim_z, True, 0)
        scale = 1.0 / 12.0
        return [
            (
                scale * (2.0 * slope[j] + (slope_up[j] + slope_down[j]) + (slope_deep[j] + slope_deep[j])),
                scale * (rim_up[j] - rim_down[j]),
                scale * (deeper[j] - shallower[j]),
            )
            for j in range(3)
        ]

    def collide_plane(j, base, grads):
        rows = pl.ds(base, SUB)
        gx, gy, gz = grads
        density, inv, reds = total[j, rows, :], inverse[j, rows, :], red[j, rows, :]
        value = [state[q, j, rows, :] for q in range(19)]
        even = {p: value[p] + value[o] for p, o in PAIRS}
        odd = {p: value[p] - value[o] for p, o in PAIRS}
        ex, ey, ez = 2.0 * even[1], 2.0 * even[3], 2.0 * even[5]
        ox, oy, oz = 2.0 * odd[1], 2.0 * odd[3], 2.0 * odd[5]
        pxy, pxz, pyz = even[7] + even[9], even[11] + even[13], even[15] + even[17]
        rxy, rxz, ryz = even[7] - even[9], even[11] - even[13], even[15] - even[17]
        x_xy, y_xy = odd[7] + odd[9], odd[7] - odd[9]
        x_xz, z_xz = odd[11] + odd[13], odd[11] - odd[13]
        y_yz, z_yz = odd[15] + odd[17], odd[15] - odd[17]
        tx, ty, tz = x_xy + x_xz, y_xy + y_yz, z_xz + z_yz
        jx, jy, jz = ox + tx, oy + ty, oz + tz
        ux, uy, uz = jx * inv, jy * inv, jz * inv
        xx, yy, zz = jx * ux, jy * uy, jz * uz
        square = xx + yy + zz
        sum_axis = ex + ey + ez
        sum_diag = pxy + pxz + pyz
        rest = 12.0 * value[0]
        d_energy = 8.0 * sum_diag - 11.0 * sum_axis - 30.0 * rest + 11.0 * density - 19.0 * square
        d_second = sum_diag - 4.0 * sum_axis + 12.0 * rest - 3.0 * density + 5.5 * square
        flat_x = 1.5 * xx - 0.5 * square
        flat_w = 0.5 * (yy - zz)
        a9 = 3.0 * ex - sum_axis - flat_x
        b9 = sum_diag - 3.0 * pyz - flat_x
        a11 = ey - ez - flat_w
        b11 = pxy - pxz - flat_w
        axis_x = (0.5 * axis_a9) * a9 + (0.5 * cross_9) * b9
        diag_x = cross_9 * a9 + diag_9 * b9
        axis_w = (0.5 * axis_a11) * a11 + (0.5 * cross_11) * b11
        diag_w = cross_11 * a11 + diag_11 * b11
        norm2 = gx * gx + gy * gy + gz * gz
        size = jnp.sqrt(norm2)
        inv_bound = 1.0 / jnp.maximum(size, gradient_floor)
        pull = (0.5 * tension) * size
        push = (0.5 * tension) * inv_bound
        iso_axis = (-5.5 * rate[1]) * d_energy - (2.0 * rate[2]) * d_second + pull
        iso_diag = (8.0 * rate[1]) * d_energy + rate[2] * d_second + pull
        iso_rest = (-2.5 * rate[1]) * d_energy + rate[2] * d_second - pull
        out_even = {
            1: iso_axis + 2.0 * axis_x,
            3: iso_axis - axis_x + axis_w,
            5: iso_axis - axis_x - axis_w,
        }
        dxy = iso_diag + diag_x + diag_w
        dxz = iso_diag + diag_x - diag_w
        dyz = iso_diag - 2.0 * diag_x
        sxy = rate[13] * (rxy - jx * uy)
        syz = rate[14] * (ryz - jy * uz)
        sxz = rate[15] * (rxz - jx * uz)
        out_even.update(
            {7: dxy + sxy, 9: dxy - sxy, 11: dxz + sxz, 13: dxz - sxz, 15: dyz + syz, 17: dyz - syz}
        )
        third = 2.0 / 3.0
        qx = rate[4] * (tx - 4.0 * ox + third * jx)
        qy = rate[6] * (ty - 4.0 * oy + third * jy)
        qz = rate[8] * (tz - 4.0 * oz + third * jz)
        mx = rate[16] * (x_xy - x_xz)
        my = rate[17] * (y_yz - y_xy)
        mz = rate[18] * (z_xz - z_yz)
        fx, fy = qx + mx, qy - my
        hx, hz = qx - mx, qz + mz
        ky, kz = qy + my, qz - mz
        out_odd = {
            1: -2.0 * qx,
            3: -2.0 * qy,
            5: -2.0 * qz,
            7: fx + fy,
            9: fx - fy,
            11: hx + hz,
            13: hx - hz,
            15: ky + kz,
            17: ky - kz,
        }
        along = {
            1: gx,
            3: gy,
            5: gz,
            7: gx + gy,
            9: gx - gy,
            11: gx + gz,
            13: gx - gz,
            15: gy + gz,
            17: gy - gz,
        }
        fraction = reds * inv
        mixing = (recolor_beta / 36.0) * reds * (1.0 - fraction)
        mix_axis = mixing * inv_bound
        mix_diag = mix_axis * float(1.0 / np.sqrt(2.0))
        relaxed = value[0] - iso_rest
        after[0, j, rows, :] = relaxed
        after[19, j, rows, :] = fraction * relaxed
        for p, o in PAIRS:
            steady = out_even[p] - (along[p] * along[p]) * push
            mixed = along[p] * (mix_axis if p < 7 else mix_diag)
            forth = value[p] - (steady + out_odd[p])
            reverse = value[o] - (steady - out_odd[p])
            after[p, j, rows, :] = forth
            after[o, j, rows, :] = reverse
            after[19 + p, j, rows, :] = fraction * forth + mixed
            after[19 + o, j, rows, :] = fraction * reverse - mixed

    def collide_rows(base):
        grads = gradient_planes(base)
        for j in range(3):
            collide_plane(j, base, grads[j])

    def stream_rows(base):
        rows = pl.ds(base, SUB)
        fluid = [rock[j, rows, :] < 0.5 for j in range(3)]
        sums = [[[], [], []], [[], [], []]]
        for q in range(19):
            a, b, c = (int(v) for v in velocity_table[q])
            back_rows = pl.ds(base - a, SUB)
            if q > 0:
                hits = [mask[q - 1, j, rows, :] > 0.5 for j in range(3)]
            for s in range(2):
                planes = [after[19 * s + q, j, back_rows, :] for j in range(3)]
                if q > 0:
                    planes = moved(planes, c % 2 == 1, b)
                    other = 19 * s + opposite_of(q)
                    planes = [
                        jnp.where(hits[j], after[other, j, rows, :], planes[j]) for j in range(3)
                    ]
                for j in range(3):
                    pltpu.store(state.at[19 * s + q, j, rows, :], planes[j], mask=fluid[j])
                    sums[s][j].append(planes[j])
        for j in range(3):
            put_macro(j, rows, weighted_sum(sums[0][j]), weighted_sum(sums[1][j]), fluid[j])

    for iteration in range(ITERS):
        width = REACH - 2 * iteration
        rows_loop(first_row - width + 1, SUB + 2 * width - 2, collide_rows)
        rows_loop(first_row - width + 2, SUB + 2 * width - 4, stream_rows)

    own = pl.ds(first_row, SUB)
    for s in range(2):
        for q in range(19):
            out_ref[s, q, 0] = state[19 * s + q, 0, own, :]
            out_ref[s, q, 1] = lane_roll(state[19 * s + q, 1, own, :], HALF)


def gather_kernel(pop_ref, lab_ref, sol_ref, out_ref):
    for member in range(19):
        for at in range(2):
            out_ref[2 * member + at] = pop_ref[member, at]
    for at in range(2):
        out_ref[38 + at] = lab_ref[at].astype(jnp.float32)
        out_ref[40 + at] = sol_ref[at].astype(jnp.float32)


def next_pairs(count):
    return [i ^ 1 for i in range(count)]


def other_pairs(count):
    return [(i + 1 if i % 2 else i - 1) % count for i in range(count)]


def far_pairs(count):
    first = [i + 2 if i % 4 < 2 else i - 2 for i in range(count)]
    second = [(i - 2 if i % 4 < 2 else i + 2) % count for i in range(count)]
    return [first] if first == second else [first, second]


def tile_spots(index, count):
    odd = index % 2
    late = (index // 2) % 2
    near = [(2,), (3 - 2 * odd,), (1 + 2 * odd,)]
    if count == 4:
        return near + [(0, 4)]
    return near + [(4 - 4 * late,), (4 * late,)]


def swapped(value, axis, partners):
    return lax.ppermute(value, axis, list(enumerate(partners)))


def vmem_call(kernel, out_shapes, args, rates=None, scratch=()):
    vmem = pl.BlockSpec(memory_space=pltpu.VMEM)
    specs = [vmem] * len(args)
    args = [pltpu.with_memory_space_constraint(arg, pltpu.VMEM) for arg in args]
    if rates is not None:
        specs.append(pl.BlockSpec(memory_space=pltpu.SMEM))
        args.append(rates)
    return pl.pallas_call(kernel, out_shape=out_shapes, in_specs=specs, scratch_shapes=scratch)(*args)


def body_deep(populations, labels, solid, rates):
    count = lax.axis_size("gx")
    main = vmem_call(
        gather_kernel, pltpu.VMEM((42, SUB, LANES), jnp.float32), [populations, labels, solid]
    )
    patterns = [next_pairs(count), other_pairs(count)] + far_pairs(count)
    mains = [main] + [swapped(main, "gx", partners) for partners in patterns]

    def edges(*refs):
        edges_kernel(refs[: len(mains)], *refs[len(mains) :])

    side = pltpu.VMEM((len(mains) * SIDE_COUNT, SUB, LANES), jnp.float32)
    inner, outer = vmem_call(edges, (side, side), mains)
    width = lax.axis_size("gy")
    inner = swapped(inner, "gy", next_pairs(width))
    outer = swapped(outer, "gy", other_pairs(width))
    rows = 5 * SUB

    def kernel(*refs):
        steps_kernel(refs[: len(mains)], *refs[len(mains) :])

    plane = pltpu.VMEM((3, rows, LANES), jnp.float32)
    return vmem_call(
        kernel,
        jax.ShapeDtypeStruct((2,) + populations.shape, jnp.float32),
        mains + [inner, outer],
        rates,
        [
            pltpu.VMEM((38, 3, rows, LANES), jnp.float32),
            pltpu.VMEM((38, 3, rows, LANES), jnp.float32),
            plane,
            plane,
            plane,
            plane,
            pltpu.VMEM((18, 3, rows, LANES), jnp.float32),
            plane,
        ],
    )


def body(populations, labels, solid, rates):
    depth, height, breadth = populations.shape[1:]
    fits = (depth, height, breadth) == (2, SUB, LANES)
    fits = fits and lax.axis_size("gx") % 4 == 0 and lax.axis_size("gy") % 2 == 0
    if fits and REACH < min(2 * SUB, SLOT):
        return body_deep(populations, labels, solid, rates)
    return body_plain(populations, labels, solid, rates)


def solution(mesh):
    return jax.shard_map(
        body,
        mesh=mesh,
        in_specs=(P(None, None, "gx", "gy"), P(None, "gx", "gy"), P(None, "gx", "gy"), P()),
        out_specs=P(None, None, None, "gx", "gy"),
        check_vma=False,
    )
```

```python
import jax
import jax.numpy as jnp
import numpy as np
from jax import lax
from jax.experimental import pallas as pl
from jax.experimental.pallas import tpu as pltpu
from jax.sharding import PartitionSpec as P

ITERS = 6


velocity_table = np.array(
    [
        [0, 0, 0],
        [1, 0, 0],
        [-1, 0, 0],
        [0, 1, 0],
        [0, -1, 0],
        [0, 0, 1],
        [0, 0, -1],
        [1, 1, 0],
        [-1, -1, 0],
        [1, -1, 0],
        [-1, 1, 0],
        [1, 0, 1],
        [-1, 0, -1],
        [1, 0, -1],
        [-1, 0, 1],
        [0, 1, 1],
        [0, -1, -1],
        [0, 1, -1],
        [0, -1, 1],
    ]
)
weight_table = np.array([1.0 / 3.0] + [1.0 / 18.0] * 6 + [1.0 / 36.0] * 12)
tension = 0.1
recolor_beta = 0.7
gradient_floor = 0.1


def padded_2(cells, sides, width):
    for axis, dim in sides:
        count = lax.axis_size(axis)
        head = lax.slice_in_dim(cells, 0, width, axis=dim)
        tail = lax.slice_in_dim(cells, cells.shape[dim] - width, cells.shape[dim], axis=dim)
        cells = jnp.concatenate(
            [
                lax.ppermute(tail, axis, [(i, (i + 1) % count) for i in range(count)]),
                cells,
                lax.ppermute(head, axis, [((i + 1) % count, i) for i in range(count)]),
            ],
            axis=dim,
        )
    return cells


def opposite_of(member):
    return int(np.argmax(np.all(velocity_table == -velocity_table[member], axis=1)))


def build_moments():
    float_table = velocity_table * 1.0
    first_axis = float_table[:, 0]
    second_axis = float_table[:, 1]
    depth_axis = float_table[:, 2]
    squared = first_axis**2 + second_axis**2 + depth_axis**2
    higher = 3.0 * squared - 5.0
    cubic = 5.0 * squared - 9.0
    first_diag = 3.0 * first_axis**2 - squared
    cross_diag = second_axis**2 - depth_axis**2
    listed = [
        squared * 0.0 + 1.0,
        19.0 * squared - 30.0,
        (21.0 * squared**2 - 53.0 * squared + 24.0) / 2.0,
        first_axis,
        cubic * first_axis,
        second_axis,
        cubic * second_axis,
        depth_axis,
        cubic * depth_axis,
        first_diag,
        higher * first_diag,
        cross_diag,
        higher * cross_diag,
        first_axis * second_axis,
        second_axis * depth_axis,
        first_axis * depth_axis,
        cross_diag * first_axis,
        (depth_axis**2 - first_axis**2) * second_axis,
        (first_axis**2 - second_axis**2) * depth_axis,
    ]
    return np.array(listed)


def build_placement():
    free_rows = [1, 2, 4, 6, 8] + list(range(9, 19))
    return np.eye(19)[free_rows]


def build_signs():
    return np.array([-1.0] + [1.0] * 18)


def build_lengths():
    return np.maximum(np.sqrt(np.sum((velocity_table * 1.0) ** 2, axis=1)), 1.0)


def lattice_tables():
    velocity = jnp.asarray(velocity_table, jnp.float32)
    weights = jnp.asarray(weight_table, jnp.float32)
    return (velocity, weights)


def relax_matrix(rates):
    moment_table = build_moments()
    inverse_table = moment_table.T / np.sum(moment_table**2, axis=1)[None, :]
    relaxation = jnp.dot(
        rates, jnp.asarray(build_placement(), jnp.float32), precision=lax.Precision.HIGHEST
    )
    inverse = jnp.asarray(inverse_table, jnp.float32)
    moment = jnp.asarray(moment_table, jnp.float32)
    matrix = jnp.dot(inverse * relaxation[None, :], moment, precision=lax.Precision.HIGHEST)
    weights = jnp.asarray(weight_table, jnp.float32)
    return matrix * weights[None, :] / weights[:, None]


def macroscopic(flattened):
    velocity, weights = lattice_tables()
    moment_rows = jnp.concatenate([weights[None, :], (velocity * weights[:, None]).T], axis=0)
    moments = jnp.dot(moment_rows, flattened[0], precision=lax.Precision.HIGHEST)
    red_mass = jnp.dot(weights[None, :], flattened[1], precision=lax.Precision.HIGHEST)
    return (moments, red_mass)


def collide(flattened, moments, red_mass, gradient, scaled):
    velocity, weights = lattice_tables()
    density = moments[0:1]
    velocity_field = moments[1:4] / density
    projected = jnp.dot(velocity, velocity_field, precision=lax.Precision.HIGHEST)
    squared_speed = jnp.sum(velocity_field * velocity_field, axis=0, keepdims=True)
    balance = density * (1.0 + 3.0 * projected + 4.5 * projected * projected - 1.5 * squared_speed)
    relaxed = flattened[0] - jnp.dot(
        scaled, flattened[0] - balance, precision=lax.Precision.HIGHEST
    )
    magnitude = jnp.sqrt(jnp.sum(gradient * gradient, axis=0, keepdims=True))
    bounded = jnp.maximum(magnitude, gradient_floor)
    aligned = jnp.dot(velocity, gradient, precision=lax.Precision.HIGHEST)
    sign_column = jnp.asarray(build_signs(), jnp.float32)[:, None]
    relaxed = relaxed + 0.5 * tension * (aligned * aligned / bounded - sign_column * magnitude)
    lengths = jnp.asarray(build_lengths(), jnp.float32)[:, None]
    fraction = red_mass / density
    mixing = recolor_beta * red_mass * (density - red_mass) / density
    recolored = fraction * relaxed + mixing * aligned / (lengths * bounded)
    return jnp.stack([relaxed, recolored])


def gradient_local(padded_phase, height, breadth):
    components = [
        jnp.zeros((padded_phase.shape[0], height, breadth), jnp.float32) for axis_number in range(3)
    ]
    for member in range(1, 19):
        along_first, along_second, along_depth = (int(value) for value in velocity_table[member])
        window = padded_phase[
            :,
            1 + along_first : 1 + along_first + height,
            1 + along_second : 1 + along_second + breadth,
        ]
        shifted = jnp.roll(window, -along_depth, axis=0)
        factor = 3.0 * float(weight_table[member])
        for axis_number, along in enumerate((along_first, along_second, along_depth)):
            if along != 0:
                components[axis_number] = components[axis_number] + factor * along * shifted
    return jnp.stack(components)


def stream_local(padded, collided, current, solid_pad, blocked, height, breadth):
    results = []
    for member in range(19):
        along_first, along_second, along_depth = (int(value) for value in velocity_table[member])
        window = padded[
            :,
            member,
            :,
            1 - along_first : 1 - along_first + height,
            1 - along_second : 1 - along_second + breadth,
        ]
        shifted = jnp.roll(window, along_depth, axis=1)
        rock_window = solid_pad[
            :,
            1 - along_first : 1 - along_first + height,
            1 - along_second : 1 - along_second + breadth,
        ]
        source_rock = jnp.roll(rock_window, along_depth, axis=0)
        bounced = collided[:, opposite_of(member)]
        pulled = jnp.where(source_rock[None], bounced, shifted)
        results.append(jnp.where(blocked[None], current[:, member], pulled))
    return jnp.stack(results, axis=1)


def body_plain(populations, labels, solid, rates):
    scaled = relax_matrix(rates)
    red_part = labels.astype(jnp.float32)[None] * populations
    current = jnp.stack([populations, red_part])
    height = populations.shape[2]
    breadth = populations.shape[3]
    blocked = solid > 0
    grid_shape = current.shape
    solid_pad = padded_2(solid, (("gx", 1), ("gy", 2)), 1) > 0
    for iteration in range(ITERS):
        flattened = current.reshape(2, 19, -1)
        moments, red_mass = macroscopic(flattened)
        phase_field = ((2.0 * red_mass - moments[0:1]) / moments[0:1]).reshape(grid_shape[2:])
        padded_phase = padded_2(phase_field, (("gx", 1), ("gy", 2)), 1)
        gradient = gradient_local(padded_phase, height, breadth).reshape(3, -1)
        collided = collide(flattened, moments, red_mass, gradient, scaled).reshape(grid_shape)
        padded = padded_2(collided, (("gx", 3), ("gy", 4)), 1)
        current = stream_local(padded, collided, current, solid_pad, blocked, height, breadth)
    return current


SUB = 8
LANES = 128
HALF = LANES // 2
SLOT = 16
REACH = 2 * ITERS
INSIDE = 32 - REACH
TURN = 2 * REACH
GROUP = 4
SIDE_COUNT = -(-21 // GROUP)
ROWS = 5 * SUB
FIRST = 2 * SUB
LAST_ROWS = 2 * SUB
PAIRS = [(m, opposite_of(m)) for m in range(1, 19) if m < opposite_of(m)]


def lane_ids(shape):
    return lax.broadcasted_iota(jnp.int32, shape, len(shape) - 1)


def within(shape, *spans):
    ids = lane_ids(shape)
    mask = None
    for first, last in spans:
        for shift in (0, HALF):
            low, high = (first + shift) % LANES, (last + shift) % LANES
            part = (ids >= low) & (ids < high) if low < high else (ids >= low) | (ids < high)
            mask = part if mask is None else mask | part
    return mask


def lane_roll(value, amount):
    return pltpu.roll(value, amount % LANES, axis=value.ndim - 1)


def moved_apart(planes, swap, along):
    if swap:
        planes = planes[::-1]
    return [lane_roll(p, along) for p in planes] if along else planes


def moved_zone(planes, swap, along):
    amount = (HALF if swap else 0) + along
    return [lane_roll(p, amount) for p in planes] if amount else planes


def moved_joined(planes, swap, along):
    first, second, side = planes
    if swap:
        first, second = second, first
    amount = (HALF if swap else 0) + along
    if amount:
        first, second, side = (lane_roll(p, amount) for p in (first, second, side))
    if along:
        ids = lane_ids(first.shape)
        edge = 0 if along > 0 else LANES - 1
        at_first = ids == edge
        at_second = ids == (edge + HALF) % LANES
        first, second, side = (
            jnp.where(at_first, side, first),
            jnp.where(at_second, side, second),
            jnp.where(at_first, first, jnp.where(at_second, second, side)),
        )
    return first, second, side


def edges_kernel(mains, inner_ref, outer_ref):
    even = lax.axis_index("gy") % 2 == 0
    low = lane_ids((SUB, LANES)) < HALF
    left_spans = [(SLOT * k, SLOT * k + REACH) for k in range(GROUP)]
    lefts = [within((SUB, LANES), span) for span in left_spans]
    rights = [within((SUB, LANES), (first - REACH, last - REACH)) for first, last in left_spans]
    deep_left = ~low
    deep_rights = [
        (lane_ids((SUB, LANES)) >= HALF - REACH + SLOT * k)
        & (lane_ids((SUB, LANES)) < LANES - REACH + SLOT * k)
        for k in range(GROUP)
    ]
    for spot, main in enumerate(mains):
        for index in range(SIDE_COUNT):
            left_all = right_all = None
            for k in range(min(GROUP, 21 - GROUP * index)):
                member = GROUP * index + k
                shallow = main[2 * member]
                if k:
                    shallow = lane_roll(shallow, SLOT * k)
                deep = lane_roll(main[2 * member + 1], HALF + SLOT * k)
                left = jnp.where(deep_left, deep, shallow)
                right = jnp.where(deep_rights[k], deep, shallow)
                left_all = left if k == 0 else jnp.where(lefts[k], left, left_all)
                right_all = right if k == 0 else jnp.where(rights[k], right, right_all)
            inner_ref[spot * SIDE_COUNT + index] = jnp.where(even, right_all, left_all)
            outer_ref[spot * SIDE_COUNT + index] = jnp.where(even, left_all, right_all)


def weighted_sum(values):
    axis = values[1]
    for q in range(2, 7):
        axis = axis + values[q]
    diag = values[7]
    for q in range(8, 19):
        diag = diag + values[q]
    return 12.0 * values[0] + 2.0 * axis + diag


class Stepper:
    pass


def make_stepper(refs, moved, rates_ref):
    state, after, phase, total, inverse, red, mask, rock = refs
    count = state.shape[1]
    stepper = Stepper()
    norms = np.sum(build_moments() ** 2, axis=1)
    free = [1, 2, 4, 6, 8] + list(range(9, 19))
    rate = {row: rates_ref[k] * float(1.0 / norms[row]) for k, row in enumerate(free)}

    def put_macro(j, rows, density, reds, where=None):
        inv = 1.0 / density
        values = ((total, density), (inverse, inv), (red, reds), (phase, (2.0 * reds - density) * inv))
        for ref, value in values:
            if where is None:
                ref[j, rows, :] = value
            else:
                pltpu.store(ref.at[j, rows, :], value, mask=where)

    def make_masks(base):
        for member in range(1, 19):
            a, b, c = (int(v) for v in velocity_table[member])
            planes = moved([rock[j, pl.ds(base - a, SUB), :] for j in range(count)], c % 2 == 1, b)
            for j in range(count):
                mask[member - 1, j, pl.ds(base, SUB), :] = planes[j]

    axis_a9 = rate[9] + 4.0 * rate[10]
    cross_9 = rate[9] - 2.0 * rate[10]
    diag_9 = rate[9] + rate[10]
    axis_a11 = rate[11] + 4.0 * rate[12]
    cross_11 = rate[11] - 2.0 * rate[12]
    diag_11 = rate[11] + rate[12]

    def gradient_planes(base):
        before = [phase[j, pl.ds(base - 1, SUB), :] for j in range(count)]
        here = [phase[j, pl.ds(base, SUB), :] for j in range(count)]
        behind = [phase[j, pl.ds(base + 1, SUB), :] for j in range(count)]
        slope = [p - m for p, m in zip(behind, before)]
        both = [p + m for p, m in zip(behind, before)]
        rim = [2.0 * h + s for h, s in zip(here, both)]
        slope_up, slope_down = moved(slope, False, -1), moved(slope, False, 1)
        slope_deep = moved(slope, True, 0)
        here_up, here_down = moved(here, False, -1), moved(here, False, 1)
        here_deep = moved(here, True, 0)
        rim_y = [r + (d + d) for r, d in zip(rim, here_deep)]
        rim_up, rim_down = moved(rim_y, False, -1), moved(rim_y, False, 1)
        rim_z = [r + (u + d) for r, u, d in zip(rim, here_up, here_down)]
        deeper, shallower = moved(rim_z, True, 0), moved(rim_z, True, 0)
        scale = 1.0 / 12.0
        return [
            (
                scale * (2.0 * slope[j] + (slope_up[j] + slope_down[j]) + (slope_deep[j] + slope_deep[j])),
                scale * (rim_up[j] - rim_down[j]),
                scale * (deeper[j] - shallower[j]),
            )
            for j in range(count)
        ]

    def collide_plane(j, base, grads):
        rows = pl.ds(base, SUB)
        gx, gy, gz = grads
        density, inv, reds = total[j, rows, :], inverse[j, rows, :], red[j, rows, :]
        value = [state[q, j, rows, :] for q in range(19)]
        even = {p: value[p] + value[o] for p, o in PAIRS}
        odd = {p: value[p] - value[o] for p, o in PAIRS}
        ex, ey, ez = 2.0 * even[1], 2.0 * even[3], 2.0 * even[5]
        ox, oy, oz = 2.0 * odd[1], 2.0 * odd[3], 2.0 * odd[5]
        pxy, pxz, pyz = even[7] + even[9], even[11] + even[13], even[15] + even[17]
        rxy, rxz, ryz = even[7] - even[9], even[11] - even[13], even[15] - even[17]
        x_xy, y_xy = odd[7] + odd[9], odd[7] - odd[9]
        x_xz, z_xz = odd[11] + odd[13], odd[11] - odd[13]
        y_yz, z_yz = odd[15] + odd[17], odd[15] - odd[17]
        tx, ty, tz = x_xy + x_xz, y_xy + y_yz, z_xz + z_yz
        jx, jy, jz = ox + tx, oy + ty, oz + tz
        ux, uy, uz = jx * inv, jy * inv, jz * inv
        xx, yy, zz = jx * ux, jy * uy, jz * uz
        square = xx + yy + zz
        sum_axis = ex + ey + ez
        sum_diag = pxy + pxz + pyz
        rest = 12.0 * value[0]
        d_energy = 8.0 * sum_diag - 11.0 * sum_axis - 30.0 * rest + 11.0 * density - 19.0 * square
        d_second = sum_diag - 4.0 * sum_axis + 12.0 * rest - 3.0 * density + 5.5 * square
        flat_x = 1.5 * xx - 0.5 * square
        flat_w = 0.5 * (yy - zz)
        a9 = 3.0 * ex - sum_axis - flat_x
        b9 = sum_diag - 3.0 * pyz - flat_x
        a11 = ey - ez - flat_w
        b11 = pxy - pxz - flat_w
        axis_x = (0.5 * axis_a9) * a9 + (0.5 * cross_9) * b9
        diag_x = cross_9 * a9 + diag_9 * b9
        axis_w = (0.5 * axis_a11) * a11 + (0.5 * cross_11) * b11
        diag_w = cross_11 * a11 + diag_11 * b11
        norm2 = gx * gx + gy * gy + gz * gz
        size = jnp.sqrt(norm2)
        inv_bound = 1.0 / jnp.maximum(size, gradient_floor)
        pull = (0.5 * tension) * size
        push = (0.5 * tension) * inv_bound
        iso_axis = (-5.5 * rate[1]) * d_energy - (2.0 * rate[2]) * d_second + pull
        iso_diag = (8.0 * rate[1]) * d_energy + rate[2] * d_second + pull
        iso_rest = (-2.5 * rate[1]) * d_energy + rate[2] * d_second - pull
        out_even = {
            1: iso_axis + 2.0 * axis_x,
            3: iso_axis - axis_x + axis_w,
            5: iso_axis - axis_x - axis_w,
        }
        dxy = iso_diag + diag_x + diag_w
        dxz = iso_diag + diag_x - diag_w
        dyz = iso_diag - 2.0 * diag_x
        sxy = rate[13] * (rxy - jx * uy)
        syz = rate[14] * (ryz - jy * uz)
        sxz = rate[15] * (rxz - jx * uz)
        out_even.update(
            {7: dxy + sxy, 9: dxy - sxy, 11: dxz + sxz, 13: dxz - sxz, 15: dyz + syz, 17: dyz - syz}
        )
        third = 2.0 / 3.0
        qx = rate[4] * (tx - 4.0 * ox + third * jx)
        qy = rate[6] * (ty - 4.0 * oy + third * jy)
        qz = rate[8] * (tz - 4.0 * oz + third * jz)
        mx = rate[16] * (x_xy - x_xz)
        my = rate[17] * (y_yz - y_xy)
        mz = rate[18] * (z_xz - z_yz)
        fx, fy = qx + mx, qy - my
        hx, hz = qx - mx, qz + mz
        ky, kz = qy + my, qz - mz
        out_odd = {
            1: -2.0 * qx,
            3: -2.0 * qy,
            5: -2.0 * qz,
            7: fx + fy,
            9: fx - fy,
            11: hx + hz,
            13: hx - hz,
            15: ky + kz,
            17: ky - kz,
        }
        along = {
            1: gx,
            3: gy,
            5: gz,
            7: gx + gy,
            9: gx - gy,
            11: gx + gz,
            13: gx - gz,
            15: gy + gz,
            17: gy - gz,
        }
        fraction = reds * inv
        mixing = (recolor_beta / 36.0) * reds * (1.0 - fraction)
        mix_axis = mixing * inv_bound
        mix_diag = mix_axis * float(1.0 / np.sqrt(2.0))
        relaxed = value[0] - iso_rest
        after[0, j, rows, :] = relaxed
        after[19, j, rows, :] = fraction * relaxed
        for p, o in PAIRS:
            steady = out_even[p] - (along[p] * along[p]) * push
            mixed = along[p] * (mix_axis if p < 7 else mix_diag)
            forth = value[p] - (steady + out_odd[p])
            reverse = value[o] - (steady - out_odd[p])
            after[p, j, rows, :] = forth
            after[o, j, rows, :] = reverse
            after[19 + p, j, rows, :] = fraction * forth + mixed
            after[19 + o, j, rows, :] = fraction * reverse - mixed

    def collide_rows(base):
        grads = gradient_planes(base)
        for j in range(count):
            collide_plane(j, base, grads[j])

    def stream_rows(base):
        rows = pl.ds(base, SUB)
        fluid = [rock[j, rows, :] < 0.5 for j in range(count)]
        sums = [[[] for j in range(count)] for s in range(2)]
        for q in range(19):
            a, b, c = (int(v) for v in velocity_table[q])
            back_rows = pl.ds(base - a, SUB)
            if q > 0:
                hits = [mask[q - 1, j, rows, :] > 0.5 for j in range(count)]
            for s in range(2):
                planes = [after[19 * s + q, j, back_rows, :] for j in range(count)]
                if q > 0:
                    planes = moved(planes, c % 2 == 1, b)
                    other = 19 * s + opposite_of(q)
                    planes = [
                        jnp.where(hits[j], after[other, j, rows, :], planes[j]) for j in range(count)
                    ]
                for j in range(count):
                    pltpu.store(state.at[19 * s + q, j, rows, :], planes[j], mask=fluid[j])
                    sums[s][j].append(planes[j])
        for j in range(count):
            put_macro(j, rows, weighted_sum(sums[0][j]), weighted_sum(sums[1][j]), fluid[j])

    def fill(values, labels, rocks, rows):
        sums = [[] for j in range(count)]
        for member in range(19):
            planes = values(member)
            for j in range(count):
                state[member, j, rows, :] = planes[j]
                state[19 + member, j, rows, :] = labels[j] * planes[j]
                sums[j].append(planes[j])
        for j in range(count):
            rock[j, rows, :] = rocks[j]
            density = weighted_sum(sums[j])
            put_macro(j, rows, density, labels[j] * density)

    def run_early():
        rows_loop(FIRST - REACH + 2, SUB + 2 * REACH - 4, make_masks)
        for iteration in range(ITERS - 1):
            width = REACH - 2 * iteration
            rows_loop(FIRST - width + 1, SUB + 2 * width - 2, collide_rows)
            rows_loop(FIRST - width + 2, SUB + 2 * width - 4, stream_rows)

    stepper.put_macro, stepper.fill, stepper.run_early = put_macro, fill, run_early
    stepper.collide_rows = collide_rows
    return stepper


def rows_loop(start, count, run):
    for index in range(-(-count // SUB)):
        run(start + index * SUB)


def tile_places(spots):
    return [pl.ds(pl.multiple_of(spot * SUB, SUB), SUB) for spot in spots]


def early_kernel(mains, rates_ref, own_ref, rock_ref, zone_ref, *scratch):
    state, rock = scratch[0], scratch[-1]
    stepper = make_stepper(scratch, moved_apart, rates_ref)
    shape = (SUB, LANES)
    ids = lane_ids(shape)
    deep = (ids >= HALF - INSIDE) & (ids < LANES - INSIDE)
    left = within(shape, (TURN, TURN + INSIDE))
    for source, (main, spots) in enumerate(zip(mains, tile_spots(lax.axis_index("gx"), len(mains)))):
        for rows in tile_places(spots):
            labels = [main[38], main[39]]
            rocks = [main[40], main[41]]
            stepper.fill(lambda member: [main[2 * member], main[2 * member + 1]], labels, rocks, rows)
        for member in range(21):
            shallow, below = main[2 * member], main[2 * member + 1]
            right_part = jnp.where(deep, lane_roll(below, HALF), shallow)
            left_part = jnp.where(ids < HALF, lane_roll(shallow, TURN), lane_roll(below, HALF + TURN))
            zone_ref[source * 21 + member] = jnp.where(left, left_part, right_part)
    stepper.run_early()
    for tile in range(LAST_ROWS // SUB):
        rows, here = pl.ds(tile * SUB, SUB), pl.ds(FIRST - 2 + tile * SUB, SUB)
        for q in range(38):
            own_ref[q, 0, rows, :] = state[q, 0, here, :]
            own_ref[q, 1, rows, :] = lane_roll(state[q, 1, here, :], HALF)
        rock_ref[0, rows, :] = rock[0, here, :]
        rock_ref[1, rows, :] = lane_roll(rock[1, here, :], HALF)


def late_kernel(
    inner_ref, outer_ref, own_ref, rock_ref, zone_ref, rates_ref, out_ref, *scratch
):
    zone_scratch, last_scratch = scratch[:8], scratch[8:]
    shape = (SUB, LANES)
    ids = lane_ids(shape)
    sources = zone_ref.shape[0] // 21
    even = lax.axis_index("gy") % 2 == 0
    zone = make_stepper(zone_scratch, moved_zone, rates_ref)
    is_ahead = within(shape, (0, REACH))
    is_behind = within(shape, (REACH, TURN))
    for source, spots in enumerate(tile_spots(lax.axis_index("gx"), sources)):
        planes = []
        for member in range(21):
            index, k = source * SIDE_COUNT + member // GROUP, member % GROUP
            if k == 0:
                inner, outer = inner_ref[index], outer_ref[index]
                ahead_pack = jnp.where(even, inner, outer)
                behind_pack = jnp.where(even, outer, inner)
            ahead = lane_roll(ahead_pack, -SLOT * k) if k else ahead_pack
            behind = lane_roll(behind_pack, TURN - SLOT * k)
            own = zone_ref[source * 21 + member]
            planes.append(jnp.where(is_ahead, ahead, jnp.where(is_behind, behind, own)))
        for rows in tile_places(spots):
            zone.fill(lambda member: [planes[member]], [planes[19]], [planes[20]], rows)
    zone.run_early()

    last = make_stepper(last_scratch, moved_joined, rates_ref)
    state, after, rock = last_scratch[0], last_scratch[1], last_scratch[-1]
    lost = 2 * (ITERS - 1)
    from_left = [(ids >= at) & (ids < at + lost) for at in (0, HALF)]
    from_right = [(ids >= at - lost) & (ids < at) for at in (LANES, HALF)]
    right_side = within(shape, (0, 32))
    for tile in range(LAST_ROWS // SUB):
        rows, here = pl.ds(tile * SUB, SUB), pl.ds(FIRST - 2 + tile * SUB, SUB)

        def joined(around, own):
            turned = lane_roll(around, -TURN)
            planes = [
                jnp.where(from_left[j], turned, jnp.where(from_right[j], around, own[j]))
                for j in range(2)
            ]
            return planes + [jnp.where(right_side, around, turned)]

        planes = joined(zone_scratch[-1][0, here, :], [rock_ref[j, rows, :] for j in range(2)])
        for j in range(3):
            rock[j, rows, :] = planes[j]
        sums = [[[] for j in range(3)] for s in range(2)]
        for q in range(38):
            own = [own_ref[q, j, rows, :] for j in range(2)]
            planes = joined(zone_scratch[0][q, 0, here, :], own)
            for j in range(3):
                state[q, j, rows, :] = planes[j]
                sums[q // 19][j].append(planes[j])
        for j in range(3):
            last.put_macro(j, rows, weighted_sum(sums[0][j]), weighted_sum(sums[1][j]))
    rows_loop(1, SUB + 2, last.collide_rows)
    rows = pl.ds(2, SUB)
    fluid = [rock[j, rows, :] < 0.5 for j in range(2)]
    for q in range(19):
        a, b, c = (int(v) for v in velocity_table[q])
        back_rows = pl.ds(2 - a, SUB)
        hits = moved_joined([rock[j, back_rows, :] for j in range(3)], c % 2 == 1, b)
        for s in range(2):
            planes = [after[19 * s + q, j, back_rows, :] for j in range(3)]
            planes = moved_joined(planes, c % 2 == 1, b)
            for j in range(2):
                value = planes[j]
                if q > 0:
                    bounced = after[19 * s + opposite_of(q), j, rows, :]
                    value = jnp.where(hits[j] > 0.5, bounced, value)
                value = jnp.where(fluid[j], value, state[19 * s + q, j, rows, :])
                out_ref[s, q, j] = lane_roll(value, HALF) if j else value


def gather_kernel(pop_ref, lab_ref, sol_ref, out_ref):
    for member in range(19):
        for at in range(2):
            out_ref[2 * member + at] = pop_ref[member, at]
    for at in range(2):
        out_ref[38 + at] = lab_ref[at].astype(jnp.float32)
        out_ref[40 + at] = sol_ref[at].astype(jnp.float32)


def next_pairs(count):
    return [i ^ 1 for i in range(count)]


def other_pairs(count):
    return [(i + 1 if i % 2 else i - 1) % count for i in range(count)]


def far_pairs(count):
    first = [i + 2 if i % 4 < 2 else i - 2 for i in range(count)]
    second = [(i - 2 if i % 4 < 2 else i + 2) % count for i in range(count)]
    return [first] if first == second else [first, second]


def tile_spots(index, count):
    odd = index % 2
    late = (index // 2) % 2
    near = [(2,), (3 - 2 * odd,), (1 + 2 * odd,)]
    if count == 4:
        return near + [(0, 4)]
    return near + [(4 - 4 * late,), (4 * late,)]


def swapped(value, axis, partners):
    return lax.ppermute(value, axis, list(enumerate(partners)))


def vmem_call(kernel, out_shapes, args, rates=None, scratch=()):
    vmem = pl.BlockSpec(memory_space=pltpu.VMEM)
    specs = [vmem] * len(args)
    args = [pltpu.with_memory_space_constraint(arg, pltpu.VMEM) for arg in args]
    if rates is not None:
        specs.append(pl.BlockSpec(memory_space=pltpu.SMEM))
        args.append(rates)
    return pl.pallas_call(kernel, out_shape=out_shapes, in_specs=specs, scratch_shapes=scratch)(*args)


def scratch_planes(count, rows):
    plane = pltpu.VMEM((count, rows, LANES), jnp.float32)
    full = pltpu.VMEM((38, count, rows, LANES), jnp.float32)
    masks = pltpu.VMEM((18, count, rows, LANES), jnp.float32)
    return [full, full, plane, plane, plane, plane, masks, plane]


def body_deep(populations, labels, solid, rates):
    high, wide = lax.axis_size("gx"), lax.axis_size("gy")
    main = pl.pallas_call(gather_kernel, out_shape=pltpu.VMEM((42, SUB, LANES), jnp.float32))(
        populations, labels, solid
    )
    patterns = [next_pairs(high), other_pairs(high)] + far_pairs(high)
    mains = [main] + [swapped(main, "gx", partners) for partners in patterns]
    number = len(mains)

    def edges(*refs):
        edges_kernel(refs[:number], *refs[number:])

    def early(*refs):
        early_kernel(refs[:number], *refs[number:])

    def planes(*shape):
        return pltpu.VMEM(shape + (LANES,), jnp.float32)

    side = planes(number * SIDE_COUNT, SUB)
    inner, outer = vmem_call(edges, (side, side), mains)
    outer = swapped(outer, "gy", other_pairs(wide))
    inner = swapped(inner, "gy", next_pairs(wide))
    kept = (planes(38, 2, LAST_ROWS), planes(2, LAST_ROWS), planes(number * 21, SUB))
    own, rock, zone = vmem_call(early, kept, mains, rates, scratch_planes(2, ROWS))
    return vmem_call(
        late_kernel,
        jax.ShapeDtypeStruct((2,) + populations.shape, jnp.float32),
        [inner, outer, own, rock, zone],
        rates,
        scratch_planes(1, ROWS) + scratch_planes(3, LAST_ROWS + SUB),
    )


def body(populations, labels, solid, rates):
    depth, height, breadth = populations.shape[1:]
    fits = (depth, height, breadth) == (2, SUB, LANES)
    fits = fits and lax.axis_size("gx") % 4 == 0 and lax.axis_size("gy") % 2 == 0
    if fits and REACH + 2 < SLOT and HALF == 2 * (REACH + INSIDE):
        return body_deep(populations, labels, solid, rates)
    return body_plain(populations, labels, solid, rates)


def solution(mesh):
    return jax.shard_map(
        body,
        mesh=mesh,
        in_specs=(P(None, None, "gx", "gy"), P(None, "gx", "gy"), P(None, "gx", "gy"), P()),
        out_specs=P(None, None, None, "gx", "gy"),
        check_vma=False,
    )
```

```python
import jax
import jax.numpy as jnp
import numpy as np
from jax import lax
from jax.experimental import pallas as pl
from jax.experimental.pallas import tpu as pltpu
from jax.sharding import PartitionSpec as P

ITERS = 6


velocity_table = np.array(
    [
        [0, 0, 0],
        [1, 0, 0],
        [-1, 0, 0],
        [0, 1, 0],
        [0, -1, 0],
        [0, 0, 1],
        [0, 0, -1],
        [1, 1, 0],
        [-1, -1, 0],
        [1, -1, 0],
        [-1, 1, 0],
        [1, 0, 1],
        [-1, 0, -1],
        [1, 0, -1],
        [-1, 0, 1],
        [0, 1, 1],
        [0, -1, -1],
        [0, 1, -1],
        [0, -1, 1],
    ]
)
weight_table = np.array([1.0 / 3.0] + [1.0 / 18.0] * 6 + [1.0 / 36.0] * 12)
tension = 0.1
recolor_beta = 0.7
gradient_floor = 0.1


def padded_2(cells, sides, width):
    for axis, dim in sides:
        count = lax.axis_size(axis)
        head = lax.slice_in_dim(cells, 0, width, axis=dim)
        tail = lax.slice_in_dim(cells, cells.shape[dim] - width, cells.shape[dim], axis=dim)
        cells = jnp.concatenate(
            [
                lax.ppermute(tail, axis, [(i, (i + 1) % count) for i in range(count)]),
                cells,
                lax.ppermute(head, axis, [((i + 1) % count, i) for i in range(count)]),
            ],
            axis=dim,
        )
    return cells


def opposite_of(member):
    return int(np.argmax(np.all(velocity_table == -velocity_table[member], axis=1)))


def build_moments():
    float_table = velocity_table * 1.0
    first_axis = float_table[:, 0]
    second_axis = float_table[:, 1]
    depth_axis = float_table[:, 2]
    squared = first_axis**2 + second_axis**2 + depth_axis**2
    higher = 3.0 * squared - 5.0
    cubic = 5.0 * squared - 9.0
    first_diag = 3.0 * first_axis**2 - squared
    cross_diag = second_axis**2 - depth_axis**2
    listed = [
        squared * 0.0 + 1.0,
        19.0 * squared - 30.0,
        (21.0 * squared**2 - 53.0 * squared + 24.0) / 2.0,
        first_axis,
        cubic * first_axis,
        second_axis,
        cubic * second_axis,
        depth_axis,
        cubic * depth_axis,
        first_diag,
        higher * first_diag,
        cross_diag,
        higher * cross_diag,
        first_axis * second_axis,
        second_axis * depth_axis,
        first_axis * depth_axis,
        cross_diag * first_axis,
        (depth_axis**2 - first_axis**2) * second_axis,
        (first_axis**2 - second_axis**2) * depth_axis,
    ]
    return np.array(listed)


def build_placement():
    free_rows = [1, 2, 4, 6, 8] + list(range(9, 19))
    return np.eye(19)[free_rows]


def build_signs():
    return np.array([-1.0] + [1.0] * 18)


def build_lengths():
    return np.maximum(np.sqrt(np.sum((velocity_table * 1.0) ** 2, axis=1)), 1.0)


def lattice_tables():
    velocity = jnp.asarray(velocity_table, jnp.float32)
    weights = jnp.asarray(weight_table, jnp.float32)
    return (velocity, weights)


def relax_matrix(rates):
    moment_table = build_moments()
    inverse_table = moment_table.T / np.sum(moment_table**2, axis=1)[None, :]
    relaxation = jnp.dot(
        rates, jnp.asarray(build_placement(), jnp.float32), precision=lax.Precision.HIGHEST
    )
    inverse = jnp.asarray(inverse_table, jnp.float32)
    moment = jnp.asarray(moment_table, jnp.float32)
    matrix = jnp.dot(inverse * relaxation[None, :], moment, precision=lax.Precision.HIGHEST)
    weights = jnp.asarray(weight_table, jnp.float32)
    return matrix * weights[None, :] / weights[:, None]


def macroscopic(flattened):
    velocity, weights = lattice_tables()
    moment_rows = jnp.concatenate([weights[None, :], (velocity * weights[:, None]).T], axis=0)
    moments = jnp.dot(moment_rows, flattened[0], precision=lax.Precision.HIGHEST)
    red_mass = jnp.dot(weights[None, :], flattened[1], precision=lax.Precision.HIGHEST)
    return (moments, red_mass)


def collide(flattened, moments, red_mass, gradient, scaled):
    velocity, _ = lattice_tables()
    density = moments[0:1]
    velocity_field = moments[1:4] / density
    projected = jnp.dot(velocity, velocity_field, precision=lax.Precision.HIGHEST)
    squared_speed = jnp.sum(velocity_field * velocity_field, axis=0, keepdims=True)
    balance = density * (1.0 + 3.0 * projected + 4.5 * projected * projected - 1.5 * squared_speed)
    relaxed = flattened[0] - jnp.dot(
        scaled, flattened[0] - balance, precision=lax.Precision.HIGHEST
    )
    magnitude = jnp.sqrt(jnp.sum(gradient * gradient, axis=0, keepdims=True))
    bounded = jnp.maximum(magnitude, gradient_floor)
    aligned = jnp.dot(velocity, gradient, precision=lax.Precision.HIGHEST)
    sign_column = jnp.asarray(build_signs(), jnp.float32)[:, None]
    relaxed = relaxed + 0.5 * tension * (aligned * aligned / bounded - sign_column * magnitude)
    lengths = jnp.asarray(build_lengths(), jnp.float32)[:, None]
    fraction = red_mass / density
    mixing = recolor_beta * red_mass * (density - red_mass) / density
    recolored = fraction * relaxed + mixing * aligned / (lengths * bounded)
    return jnp.stack([relaxed, recolored])


def gradient_local(padded_phase, height, breadth):
    components = [
        jnp.zeros((padded_phase.shape[0], height, breadth), jnp.float32) for _ in range(3)
    ]
    for member in range(1, 19):
        along_first, along_second, along_depth = (int(value) for value in velocity_table[member])
        window = padded_phase[
            :,
            1 + along_first : 1 + along_first + height,
            1 + along_second : 1 + along_second + breadth,
        ]
        shifted = jnp.roll(window, -along_depth, axis=0)
        factor = 3.0 * float(weight_table[member])
        for axis_number, along in enumerate((along_first, along_second, along_depth)):
            if along != 0:
                components[axis_number] = components[axis_number] + factor * along * shifted
    return jnp.stack(components)


def stream_local(padded, collided, current, solid_pad, blocked, height, breadth):
    results = []
    for member in range(19):
        along_first, along_second, along_depth = (int(value) for value in velocity_table[member])
        window = padded[
            :,
            member,
            :,
            1 - along_first : 1 - along_first + height,
            1 - along_second : 1 - along_second + breadth,
        ]
        shifted = jnp.roll(window, along_depth, axis=1)
        rock_window = solid_pad[
            :,
            1 - along_first : 1 - along_first + height,
            1 - along_second : 1 - along_second + breadth,
        ]
        source_rock = jnp.roll(rock_window, along_depth, axis=0)
        bounced = collided[:, opposite_of(member)]
        pulled = jnp.where(source_rock[None], bounced, shifted)
        results.append(jnp.where(blocked[None], current[:, member], pulled))
    return jnp.stack(results, axis=1)


def body_plain(populations, labels, solid, rates):
    scaled = relax_matrix(rates)
    red_part = labels.astype(jnp.float32)[None] * populations
    current = jnp.stack([populations, red_part])
    height = populations.shape[2]
    breadth = populations.shape[3]
    blocked = solid > 0
    grid_shape = current.shape
    solid_pad = padded_2(solid, (("gx", 1), ("gy", 2)), 1) > 0
    for _ in range(ITERS):
        flattened = current.reshape(2, 19, -1)
        moments, red_mass = macroscopic(flattened)
        phase_field = ((2.0 * red_mass - moments[0:1]) / moments[0:1]).reshape(grid_shape[2:])
        padded_phase = padded_2(phase_field, (("gx", 1), ("gy", 2)), 1)
        gradient = gradient_local(padded_phase, height, breadth).reshape(3, -1)
        collided = collide(flattened, moments, red_mass, gradient, scaled).reshape(grid_shape)
        padded = padded_2(collided, (("gx", 3), ("gy", 4)), 1)
        current = stream_local(padded, collided, current, solid_pad, blocked, height, breadth)
    return current


SUB = 8
LANES = 128
HALF = LANES // 2
SLOT = 16
REACH = 2 * ITERS
INSIDE = 32 - REACH
TURN = 2 * REACH
GROUP = 4
SIDE_COUNT = -(-21 // GROUP)
ROWS = 5 * SUB
FIRST = 2 * SUB
LAST_ROWS = 2 * SUB
PAIRS = [(m, opposite_of(m)) for m in range(1, 19) if m < opposite_of(m)]


def lane_ids(shape):
    return lax.broadcasted_iota(jnp.int32, shape, len(shape) - 1)


def within(shape, *spans):
    ids = lane_ids(shape)
    mask = None
    for first, last in spans:
        for shift in (0, HALF):
            low, high = (first + shift) % LANES, (last + shift) % LANES
            part = (ids >= low) & (ids < high) if low < high else (ids >= low) | (ids < high)
            mask = part if mask is None else mask | part
    return mask


def lane_roll(value, amount):
    return pltpu.roll(value, amount % LANES, axis=value.ndim - 1)


def moved_apart(planes, swap, along):
    if swap:
        planes = planes[::-1]
    return [lane_roll(p, along) for p in planes] if along else planes


def moved_zone(planes, swap, along):
    amount = (HALF if swap else 0) + along
    return [lane_roll(p, amount) for p in planes] if amount else planes


def moved_joined(planes, swap, along):
    first, second, side = planes
    if swap:
        first, second = second, first
    amount = (HALF if swap else 0) + along
    if amount:
        first, second, side = (lane_roll(p, amount) for p in (first, second, side))
    if along:
        ids = lane_ids(first.shape)
        edge = 0 if along > 0 else LANES - 1
        at_first = ids == edge
        at_second = ids == (edge + HALF) % LANES
        first, second, side = (
            jnp.where(at_first, side, first),
            jnp.where(at_second, side, second),
            jnp.where(at_first, first, jnp.where(at_second, second, side)),
        )
    return first, second, side


def gather_kernel(pop_ref, lab_ref, sol_ref, main, inner_ref, outer_ref):
    for member in range(19):
        for at in range(2):
            main[2 * member + at] = pop_ref[member, at]
    for at in range(2):
        main[38 + at] = lab_ref[at].astype(jnp.float32)
        main[40 + at] = sol_ref[at].astype(jnp.float32)
    even = lax.axis_index("gy") % 2 == 0
    low = lane_ids((SUB, LANES)) < HALF
    left_spans = [(SLOT * k, SLOT * k + REACH) for k in range(GROUP)]
    lefts = [within((SUB, LANES), span) for span in left_spans]
    rights = [within((SUB, LANES), (first - REACH, last - REACH)) for first, last in left_spans]
    deep_left = ~low
    deep_rights = [
        (lane_ids((SUB, LANES)) >= HALF - REACH + SLOT * k)
        & (lane_ids((SUB, LANES)) < LANES - REACH + SLOT * k)
        for k in range(GROUP)
    ]
    for index in range(SIDE_COUNT):
        left_all = right_all = None
        for k in range(min(GROUP, 21 - GROUP * index)):
            member = GROUP * index + k
            shallow = main[2 * member]
            if k:
                shallow = lane_roll(shallow, SLOT * k)
            deep = lane_roll(main[2 * member + 1], HALF + SLOT * k)
            left = jnp.where(deep_left, deep, shallow)
            right = jnp.where(deep_rights[k], deep, shallow)
            left_all = left if k == 0 else jnp.where(lefts[k], left, left_all)
            right_all = right if k == 0 else jnp.where(rights[k], right, right_all)
        inner_ref[index] = jnp.where(even, right_all, left_all)
        outer_ref[index] = jnp.where(even, left_all, right_all)


def weighted_sum(values):
    axis = values[1]
    for q in range(2, 7):
        axis = axis + values[q]
    diag = values[7]
    for q in range(8, 19):
        diag = diag + values[q]
    return 12.0 * values[0] + 2.0 * axis + diag


class Stepper:
    pass


def make_stepper(refs, moved, rates_ref):
    state, after, phase, total, inverse, red, mask, rock = refs
    count = state.shape[1]
    stepper = Stepper()
    norms = np.sum(build_moments() ** 2, axis=1)
    free = [1, 2, 4, 6, 8] + list(range(9, 19))
    rate = {row: rates_ref[k] * float(1.0 / norms[row]) for k, row in enumerate(free)}

    def put_macro(j, rows, density, reds, where=None):
        inv = 1.0 / density
        values = ((total, density), (inverse, inv), (red, reds), (phase, (2.0 * reds - density) * inv))
        for ref, value in values:
            if where is None:
                ref[j, rows, :] = value
            else:
                pltpu.store(ref.at[j, rows, :], value, mask=where)

    def make_masks(base):
        for member in range(1, 19):
            a, b, c = (int(v) for v in velocity_table[member])
            planes = moved([rock[j, pl.ds(base - a, SUB), :] for j in range(count)], c % 2 == 1, b)
            for j in range(count):
                mask[member - 1, j, pl.ds(base, SUB), :] = planes[j]

    axis_a9 = rate[9] + 4.0 * rate[10]
    cross_9 = rate[9] - 2.0 * rate[10]
    diag_9 = rate[9] + rate[10]
    axis_a11 = rate[11] + 4.0 * rate[12]
    cross_11 = rate[11] - 2.0 * rate[12]
    diag_11 = rate[11] + rate[12]

    def gradient_planes(base):
        before = [phase[j, pl.ds(base - 1, SUB), :] for j in range(count)]
        here = [phase[j, pl.ds(base, SUB), :] for j in range(count)]
        behind = [phase[j, pl.ds(base + 1, SUB), :] for j in range(count)]
        slope = [p - m for p, m in zip(behind, before)]
        both = [p + m for p, m in zip(behind, before)]
        rim = [2.0 * h + s for h, s in zip(here, both)]
        slope_up, slope_down = moved(slope, False, -1), moved(slope, False, 1)
        slope_deep = moved(slope, True, 0)
        here_up, here_down = moved(here, False, -1), moved(here, False, 1)
        here_deep = moved(here, True, 0)
        rim_y = [r + (d + d) for r, d in zip(rim, here_deep)]
        rim_up, rim_down = moved(rim_y, False, -1), moved(rim_y, False, 1)
        rim_z = [r + (u + d) for r, u, d in zip(rim, here_up, here_down)]
        deeper, shallower = moved(rim_z, True, 0), moved(rim_z, True, 0)
        scale = 1.0 / 12.0
        return [
            (
                scale * (2.0 * slope[j] + (slope_up[j] + slope_down[j]) + (slope_deep[j] + slope_deep[j])),
                scale * (rim_up[j] - rim_down[j]),
                scale * (deeper[j] - shallower[j]),
            )
            for j in range(count)
        ]

    def collide_plane(j, base, grads):
        rows = pl.ds(base, SUB)
        gx, gy, gz = grads
        density, inv, reds = total[j, rows, :], inverse[j, rows, :], red[j, rows, :]
        value = [state[q, j, rows, :] for q in range(19)]
        even = {p: value[p] + value[o] for p, o in PAIRS}
        odd = {p: value[p] - value[o] for p, o in PAIRS}
        ex, ey, ez = 2.0 * even[1], 2.0 * even[3], 2.0 * even[5]
        ox, oy, oz = 2.0 * odd[1], 2.0 * odd[3], 2.0 * odd[5]
        pxy, pxz, pyz = even[7] + even[9], even[11] + even[13], even[15] + even[17]
        rxy, rxz, ryz = even[7] - even[9], even[11] - even[13], even[15] - even[17]
        x_xy, y_xy = odd[7] + odd[9], odd[7] - odd[9]
        x_xz, z_xz = odd[11] + odd[13], odd[11] - odd[13]
        y_yz, z_yz = odd[15] + odd[17], odd[15] - odd[17]
        tx, ty, tz = x_xy + x_xz, y_xy + y_yz, z_xz + z_yz
        jx, jy, jz = ox + tx, oy + ty, oz + tz
        ux, uy, uz = jx * inv, jy * inv, jz * inv
        xx, yy, zz = jx * ux, jy * uy, jz * uz
        square = xx + yy + zz
        sum_axis = ex + ey + ez
        sum_diag = pxy + pxz + pyz
        rest = 12.0 * value[0]
        d_energy = 8.0 * sum_diag - 11.0 * sum_axis - 30.0 * rest + 11.0 * density - 19.0 * square
        d_second = sum_diag - 4.0 * sum_axis + 12.0 * rest - 3.0 * density + 5.5 * square
        flat_x = 1.5 * xx - 0.5 * square
        flat_w = 0.5 * (yy - zz)
        a9 = 3.0 * ex - sum_axis - flat_x
        b9 = sum_diag - 3.0 * pyz - flat_x
        a11 = ey - ez - flat_w
        b11 = pxy - pxz - flat_w
        axis_x = (0.5 * axis_a9) * a9 + (0.5 * cross_9) * b9
        diag_x = cross_9 * a9 + diag_9 * b9
        axis_w = (0.5 * axis_a11) * a11 + (0.5 * cross_11) * b11
        diag_w = cross_11 * a11 + diag_11 * b11
        norm2 = gx * gx + gy * gy + gz * gz
        size = jnp.sqrt(norm2)
        inv_bound = 1.0 / jnp.maximum(size, gradient_floor)
        pull = (0.5 * tension) * size
        push = (0.5 * tension) * inv_bound
        iso_axis = (-5.5 * rate[1]) * d_energy - (2.0 * rate[2]) * d_second + pull
        iso_diag = (8.0 * rate[1]) * d_energy + rate[2] * d_second + pull
        iso_rest = (-2.5 * rate[1]) * d_energy + rate[2] * d_second - pull
        out_even = {
            1: iso_axis + 2.0 * axis_x,
            3: iso_axis - axis_x + axis_w,
            5: iso_axis - axis_x - axis_w,
        }
        dxy = iso_diag + diag_x + diag_w
        dxz = iso_diag + diag_x - diag_w
        dyz = iso_diag - 2.0 * diag_x
        sxy = rate[13] * (rxy - jx * uy)
        syz = rate[14] * (ryz - jy * uz)
        sxz = rate[15] * (rxz - jx * uz)
        out_even.update(
            {7: dxy + sxy, 9: dxy - sxy, 11: dxz + sxz, 13: dxz - sxz, 15: dyz + syz, 17: dyz - syz}
        )
        third = 2.0 / 3.0
        qx = rate[4] * (tx - 4.0 * ox + third * jx)
        qy = rate[6] * (ty - 4.0 * oy + third * jy)
        qz = rate[8] * (tz - 4.0 * oz + third * jz)
        mx = rate[16] * (x_xy - x_xz)
        my = rate[17] * (y_yz - y_xy)
        mz = rate[18] * (z_xz - z_yz)
        fx, fy = qx + mx, qy - my
        hx, hz = qx - mx, qz + mz
        ky, kz = qy + my, qz - mz
        out_odd = {
            1: -2.0 * qx,
            3: -2.0 * qy,
            5: -2.0 * qz,
            7: fx + fy,
            9: fx - fy,
            11: hx + hz,
            13: hx - hz,
            15: ky + kz,
            17: ky - kz,
        }
        along = {
            1: gx,
            3: gy,
            5: gz,
            7: gx + gy,
            9: gx - gy,
            11: gx + gz,
            13: gx - gz,
            15: gy + gz,
            17: gy - gz,
        }
        fraction = reds * inv
        mixing = (recolor_beta / 36.0) * reds * (1.0 - fraction)
        mix_axis = mixing * inv_bound
        mix_diag = mix_axis * float(1.0 / np.sqrt(2.0))
        relaxed = value[0] - iso_rest
        after[0, j, rows, :] = relaxed
        after[19, j, rows, :] = fraction * relaxed
        for p, o in PAIRS:
            steady = out_even[p] - (along[p] * along[p]) * push
            mixed = along[p] * (mix_axis if p < 7 else mix_diag)
            forth = value[p] - (steady + out_odd[p])
            reverse = value[o] - (steady - out_odd[p])
            after[p, j, rows, :] = forth
            after[o, j, rows, :] = reverse
            after[19 + p, j, rows, :] = fraction * forth + mixed
            after[19 + o, j, rows, :] = fraction * reverse - mixed

    def collide_rows(base):
        grads = gradient_planes(base)
        for j in range(count):
            collide_plane(j, base, grads[j])

    def stream_rows(base):
        rows = pl.ds(base, SUB)
        fluid = [rock[j, rows, :] < 0.5 for j in range(count)]
        sums = [[[] for _ in range(count)] for _ in range(2)]
        for q in range(19):
            a, b, c = (int(v) for v in velocity_table[q])
            back_rows = pl.ds(base - a, SUB)
            if q > 0:
                hits = [mask[q - 1, j, rows, :] > 0.5 for j in range(count)]
            for s in range(2):
                planes = [after[19 * s + q, j, back_rows, :] for j in range(count)]
                if q > 0:
                    planes = moved(planes, c % 2 == 1, b)
                    other = 19 * s + opposite_of(q)
                    planes = [
                        jnp.where(hits[j], after[other, j, rows, :], planes[j]) for j in range(count)
                    ]
                for j in range(count):
                    pltpu.store(state.at[19 * s + q, j, rows, :], planes[j], mask=fluid[j])
                    sums[s][j].append(planes[j])
        for j in range(count):
            put_macro(j, rows, weighted_sum(sums[0][j]), weighted_sum(sums[1][j]), fluid[j])

    def fill(values, labels, rocks, rows):
        sums = [[] for _ in range(count)]
        for member in range(19):
            planes = values(member)
            for j in range(count):
                state[member, j, rows, :] = planes[j]
                state[19 + member, j, rows, :] = labels[j] * planes[j]
                sums[j].append(planes[j])
        for j in range(count):
            rock[j, rows, :] = rocks[j]
            density = weighted_sum(sums[j])
            put_macro(j, rows, density, labels[j] * density)

    def run_early():
        rows_loop(FIRST - REACH + 2, SUB + 2 * REACH - 4, make_masks)
        for iteration in range(ITERS - 1):
            width = REACH - 2 * iteration
            rows_loop(FIRST - width + 1, SUB + 2 * width - 2, collide_rows)
            rows_loop(FIRST - width + 2, SUB + 2 * width - 4, stream_rows)

    stepper.put_macro, stepper.fill, stepper.run_early = put_macro, fill, run_early
    stepper.collide_rows = collide_rows
    return stepper


def rows_loop(start, count, run):
    for index in range(-(-count // SUB)):
        run(start + index * SUB)


def tile_places(spots):
    return [pl.ds(pl.multiple_of(spot * SUB, SUB), SUB) for spot in spots]


def early_kernel(mains, rates_ref, own_ref, rock_ref, zone_ref, *scratch):
    state, rock = scratch[0], scratch[-1]
    stepper = make_stepper(scratch, moved_apart, rates_ref)
    shape = (SUB, LANES)
    ids = lane_ids(shape)
    deep = (ids >= HALF - INSIDE) & (ids < LANES - INSIDE)
    left = within(shape, (TURN, TURN + INSIDE))
    for source, (main, spots) in enumerate(zip(mains, tile_spots(lax.axis_index("gx"), len(mains)))):
        for rows in tile_places(spots):
            labels = [main[38], main[39]]
            rocks = [main[40], main[41]]
            stepper.fill(lambda member: [main[2 * member], main[2 * member + 1]], labels, rocks, rows)
        for member in range(21):
            shallow, below = main[2 * member], main[2 * member + 1]
            right_part = jnp.where(deep, lane_roll(below, HALF), shallow)
            left_part = jnp.where(ids < HALF, lane_roll(shallow, TURN), lane_roll(below, HALF + TURN))
            zone_ref[source * 21 + member] = jnp.where(left, left_part, right_part)
    stepper.run_early()
    for tile in range(LAST_ROWS // SUB):
        rows, here = pl.ds(tile * SUB, SUB), pl.ds(FIRST - 2 + tile * SUB, SUB)
        for q in range(38):
            own_ref[q, 0, rows, :] = state[q, 0, here, :]
            own_ref[q, 1, rows, :] = lane_roll(state[q, 1, here, :], HALF)
        rock_ref[0, rows, :] = rock[0, here, :]
        rock_ref[1, rows, :] = lane_roll(rock[1, here, :], HALF)


def late_kernel(sides, own_ref, rock_ref, zone_ref, rates_ref, out_ref, *scratch):
    zone_scratch, last_scratch = scratch[:8], scratch[8:]
    shape = (SUB, LANES)
    ids = lane_ids(shape)
    sources = zone_ref.shape[0] // 21
    even = lax.axis_index("gy") % 2 == 0
    zone = make_stepper(zone_scratch, moved_zone, rates_ref)
    is_ahead = within(shape, (0, REACH))
    is_behind = within(shape, (REACH, TURN))
    for source, spots in enumerate(tile_spots(lax.axis_index("gx"), sources)):
        planes = []
        for member in range(21):
            index, k = member // GROUP, member % GROUP
            if k == 0:
                inner, outer = sides[source][index], sides[source][SIDE_COUNT + index]
                ahead_pack = jnp.where(even, inner, outer)
                behind_pack = jnp.where(even, outer, inner)
            ahead = lane_roll(ahead_pack, -SLOT * k) if k else ahead_pack
            behind = lane_roll(behind_pack, TURN - SLOT * k)
            own = zone_ref[source * 21 + member]
            planes.append(jnp.where(is_ahead, ahead, jnp.where(is_behind, behind, own)))
        for rows in tile_places(spots):
            zone.fill(lambda member: [planes[member]], [planes[19]], [planes[20]], rows)
    zone.run_early()

    last = make_stepper(last_scratch, moved_joined, rates_ref)
    state, after, rock = last_scratch[0], last_scratch[1], last_scratch[-1]
    lost = 2 * (ITERS - 1)
    from_left = [(ids >= at) & (ids < at + lost) for at in (0, HALF)]
    from_right = [(ids >= at - lost) & (ids < at) for at in (LANES, HALF)]
    right_side = within(shape, (0, 32))
    for tile in range(LAST_ROWS // SUB):
        rows, here = pl.ds(tile * SUB, SUB), pl.ds(FIRST - 2 + tile * SUB, SUB)

        def joined(around, own):
            turned = lane_roll(around, -TURN)
            planes = [
                jnp.where(from_left[j], turned, jnp.where(from_right[j], around, own[j]))
                for j in range(2)
            ]
            return planes + [jnp.where(right_side, around, turned)]

        planes = joined(zone_scratch[-1][0, here, :], [rock_ref[j, rows, :] for j in range(2)])
        for j in range(3):
            rock[j, rows, :] = planes[j]
        sums = [[[] for _ in range(3)] for _ in range(2)]
        for q in range(38):
            own = [own_ref[q, j, rows, :] for j in range(2)]
            planes = joined(zone_scratch[0][q, 0, here, :], own)
            for j in range(3):
                state[q, j, rows, :] = planes[j]
                sums[q // 19][j].append(planes[j])
        for j in range(3):
            last.put_macro(j, rows, weighted_sum(sums[0][j]), weighted_sum(sums[1][j]))
    rows_loop(1, SUB + 2, last.collide_rows)
    rows = pl.ds(2, SUB)
    fluid = [rock[j, rows, :] < 0.5 for j in range(2)]
    for q in range(19):
        a, b, c = (int(v) for v in velocity_table[q])
        back_rows = pl.ds(2 - a, SUB)
        hits = moved_joined([rock[j, back_rows, :] for j in range(3)], c % 2 == 1, b)
        for s in range(2):
            planes = [after[19 * s + q, j, back_rows, :] for j in range(3)]
            planes = moved_joined(planes, c % 2 == 1, b)
            for j in range(2):
                value = planes[j]
                if q > 0:
                    bounced = after[19 * s + opposite_of(q), j, rows, :]
                    value = jnp.where(hits[j] > 0.5, bounced, value)
                value = jnp.where(fluid[j], value, state[19 * s + q, j, rows, :])
                out_ref[s, q, j] = lane_roll(value, HALF) if j else value


def next_pairs(count):
    return [i ^ 1 for i in range(count)]


def other_pairs(count):
    return [(i + 1 if i % 2 else i - 1) % count for i in range(count)]


def far_pairs(count):
    first = [i + 2 if i % 4 < 2 else i - 2 for i in range(count)]
    second = [(i - 2 if i % 4 < 2 else i + 2) % count for i in range(count)]
    return [first] if first == second else [first, second]


def tile_spots(index, count):
    odd = index % 2
    late = (index // 2) % 2
    near = [(2,), (3 - 2 * odd,), (1 + 2 * odd,)]
    if count == 4:
        return near + [(0, 4)]
    return near + [(4 - 4 * late,), (4 * late,)]


def swapped(value, axis, partners):
    return lax.ppermute(value, axis, list(enumerate(partners)))


def vmem_call(kernel, out_shapes, args, rates=None, scratch=()):
    vmem = pl.BlockSpec(memory_space=pltpu.VMEM)
    specs = [vmem] * len(args)
    args = [pltpu.with_memory_space_constraint(arg, pltpu.VMEM) for arg in args]
    if rates is not None:
        specs.append(pl.BlockSpec(memory_space=pltpu.SMEM))
        args.append(rates)
    return pl.pallas_call(kernel, out_shape=out_shapes, in_specs=specs, scratch_shapes=scratch)(*args)


def scratch_planes(count, rows):
    plane = pltpu.VMEM((count, rows, LANES), jnp.float32)
    full = pltpu.VMEM((38, count, rows, LANES), jnp.float32)
    masks = pltpu.VMEM((18, count, rows, LANES), jnp.float32)
    return [full, full, plane, plane, plane, plane, masks, plane]


def body_deep(populations, labels, solid, rates):
    high, wide = lax.axis_size("gx"), lax.axis_size("gy")
    patterns = [next_pairs(high), other_pairs(high)] + far_pairs(high)
    number = 1 + len(patterns)

    def planes(*shape):
        return pltpu.VMEM(shape + (LANES,), jnp.float32)

    def early(*refs):
        early_kernel(refs[:number], *refs[number:])

    def late(*refs):
        late_kernel(refs[:number], *refs[number:])

    border = planes(SIDE_COUNT, SUB)
    main, inner, outer = pl.pallas_call(gather_kernel, out_shape=(planes(42, SUB), border, border))(
        populations, labels, solid
    )
    mains = [main] + [swapped(main, "gx", partners) for partners in patterns]
    outer = swapped(outer, "gy", other_pairs(wide))
    inner = swapped(inner, "gy", next_pairs(wide))
    side = jnp.concatenate([inner, outer], axis=0)
    sides = [side] + [swapped(side, "gx", partners) for partners in patterns]
    kept = (planes(38, 2, LAST_ROWS), planes(2, LAST_ROWS), planes(number * 21, SUB))
    own, rock, zone = vmem_call(early, kept, mains, rates, scratch_planes(2, ROWS))
    return vmem_call(
        late,
        jax.ShapeDtypeStruct((2,) + populations.shape, jnp.float32),
        sides + [own, rock, zone],
        rates,
        scratch_planes(1, ROWS) + scratch_planes(3, LAST_ROWS + SUB),
    )


def body(populations, labels, solid, rates):
    depth, height, breadth = populations.shape[1:]
    fits = (depth, height, breadth) == (2, SUB, LANES)
    fits = fits and lax.axis_size("gx") % 4 == 0 and lax.axis_size("gy") % 2 == 0
    if fits and REACH + 2 < SLOT and HALF == 2 * (REACH + INSIDE):
        return body_deep(populations, labels, solid, rates)
    return body_plain(populations, labels, solid, rates)


def solution(mesh):
    return jax.shard_map(
        body,
        mesh=mesh,
        in_specs=(P(None, None, "gx", "gy"), P(None, "gx", "gy"), P(None, "gx", "gy"), P()),
        out_specs=P(None, None, None, "gx", "gy"),
        check_vma=False,
    )
```

```python
import jax
import jax.numpy as jnp
import numpy as np
from jax import lax
from jax.experimental import pallas as pl
from jax.experimental.pallas import tpu as pltpu
from jax.sharding import PartitionSpec as P

ITERS = 6


velocity_table = np.array(
    [
        [0, 0, 0],
        [1, 0, 0],
        [-1, 0, 0],
        [0, 1, 0],
        [0, -1, 0],
        [0, 0, 1],
        [0, 0, -1],
        [1, 1, 0],
        [-1, -1, 0],
        [1, -1, 0],
        [-1, 1, 0],
        [1, 0, 1],
        [-1, 0, -1],
        [1, 0, -1],
        [-1, 0, 1],
        [0, 1, 1],
        [0, -1, -1],
        [0, 1, -1],
        [0, -1, 1],
    ]
)
weight_table = np.array([1.0 / 3.0] + [1.0 / 18.0] * 6 + [1.0 / 36.0] * 12)
tension = 0.1
recolor_beta = 0.7
gradient_floor = 0.1


def padded_2(cells, sides, width):
    for axis, dim in sides:
        count = lax.axis_size(axis)
        head = lax.slice_in_dim(cells, 0, width, axis=dim)
        tail = lax.slice_in_dim(cells, cells.shape[dim] - width, cells.shape[dim], axis=dim)
        cells = jnp.concatenate(
            [
                lax.ppermute(tail, axis, [(i, (i + 1) % count) for i in range(count)]),
                cells,
                lax.ppermute(head, axis, [((i + 1) % count, i) for i in range(count)]),
            ],
            axis=dim,
        )
    return cells


def opposite_of(member):
    return int(np.argmax(np.all(velocity_table == -velocity_table[member], axis=1)))


def build_moments():
    float_table = velocity_table * 1.0
    first_axis = float_table[:, 0]
    second_axis = float_table[:, 1]
    depth_axis = float_table[:, 2]
    squared = first_axis**2 + second_axis**2 + depth_axis**2
    higher = 3.0 * squared - 5.0
    cubic = 5.0 * squared - 9.0
    first_diag = 3.0 * first_axis**2 - squared
    cross_diag = second_axis**2 - depth_axis**2
    listed = [
        squared * 0.0 + 1.0,
        19.0 * squared - 30.0,
        (21.0 * squared**2 - 53.0 * squared + 24.0) / 2.0,
        first_axis,
        cubic * first_axis,
        second_axis,
        cubic * second_axis,
        depth_axis,
        cubic * depth_axis,
        first_diag,
        higher * first_diag,
        cross_diag,
        higher * cross_diag,
        first_axis * second_axis,
        second_axis * depth_axis,
        first_axis * depth_axis,
        cross_diag * first_axis,
        (depth_axis**2 - first_axis**2) * second_axis,
        (first_axis**2 - second_axis**2) * depth_axis,
    ]
    return np.array(listed)


def build_placement():
    free_rows = [1, 2, 4, 6, 8] + list(range(9, 19))
    return np.eye(19)[free_rows]


def build_signs():
    return np.array([-1.0] + [1.0] * 18)


def build_lengths():
    return np.maximum(np.sqrt(np.sum((velocity_table * 1.0) ** 2, axis=1)), 1.0)


def lattice_tables():
    velocity = jnp.asarray(velocity_table, jnp.float32)
    weights = jnp.asarray(weight_table, jnp.float32)
    return (velocity, weights)


def relax_matrix(rates):
    moment_table = build_moments()
    inverse_table = moment_table.T / np.sum(moment_table**2, axis=1)[None, :]
    relaxation = jnp.dot(
        rates, jnp.asarray(build_placement(), jnp.float32), precision=lax.Precision.HIGHEST
    )
    inverse = jnp.asarray(inverse_table, jnp.float32)
    moment = jnp.asarray(moment_table, jnp.float32)
    matrix = jnp.dot(inverse * relaxation[None, :], moment, precision=lax.Precision.HIGHEST)
    weights = jnp.asarray(weight_table, jnp.float32)
    return matrix * weights[None, :] / weights[:, None]


def macroscopic(flattened):
    velocity, weights = lattice_tables()
    moment_rows = jnp.concatenate([weights[None, :], (velocity * weights[:, None]).T], axis=0)
    moments = jnp.dot(moment_rows, flattened[0], precision=lax.Precision.HIGHEST)
    red_mass = jnp.dot(weights[None, :], flattened[1], precision=lax.Precision.HIGHEST)
    return (moments, red_mass)


def collide(flattened, moments, red_mass, gradient, scaled):
    velocity, _ = lattice_tables()
    density = moments[0:1]
    velocity_field = moments[1:4] / density
    projected = jnp.dot(velocity, velocity_field, precision=lax.Precision.HIGHEST)
    squared_speed = jnp.sum(velocity_field * velocity_field, axis=0, keepdims=True)
    balance = density * (1.0 + 3.0 * projected + 4.5 * projected * projected - 1.5 * squared_speed)
    relaxed = flattened[0] - jnp.dot(
        scaled, flattened[0] - balance, precision=lax.Precision.HIGHEST
    )
    magnitude = jnp.sqrt(jnp.sum(gradient * gradient, axis=0, keepdims=True))
    bounded = jnp.maximum(magnitude, gradient_floor)
    aligned = jnp.dot(velocity, gradient, precision=lax.Precision.HIGHEST)
    sign_column = jnp.asarray(build_signs(), jnp.float32)[:, None]
    relaxed = relaxed + 0.5 * tension * (aligned * aligned / bounded - sign_column * magnitude)
    lengths = jnp.asarray(build_lengths(), jnp.float32)[:, None]
    fraction = red_mass / density
    mixing = recolor_beta * red_mass * (density - red_mass) / density
    recolored = fraction * relaxed + mixing * aligned / (lengths * bounded)
    return jnp.stack([relaxed, recolored])


def gradient_local(padded_phase, height, breadth):
    components = [
        jnp.zeros((padded_phase.shape[0], height, breadth), jnp.float32) for _ in range(3)
    ]
    for member in range(1, 19):
        along_first, along_second, along_depth = (int(value) for value in velocity_table[member])
        window = padded_phase[
            :,
            1 + along_first : 1 + along_first + height,
            1 + along_second : 1 + along_second + breadth,
        ]
        shifted = jnp.roll(window, -along_depth, axis=0)
        factor = 3.0 * float(weight_table[member])
        for axis_number, along in enumerate((along_first, along_second, along_depth)):
            if along != 0:
                components[axis_number] = components[axis_number] + factor * along * shifted
    return jnp.stack(components)


def stream_local(padded, collided, current, solid_pad, blocked, height, breadth):
    results = []
    for member in range(19):
        along_first, along_second, along_depth = (int(value) for value in velocity_table[member])
        window = padded[
            :,
            member,
            :,
            1 - along_first : 1 - along_first + height,
            1 - along_second : 1 - along_second + breadth,
        ]
        shifted = jnp.roll(window, along_depth, axis=1)
        rock_window = solid_pad[
            :,
            1 - along_first : 1 - along_first + height,
            1 - along_second : 1 - along_second + breadth,
        ]
        source_rock = jnp.roll(rock_window, along_depth, axis=0)
        bounced = collided[:, opposite_of(member)]
        pulled = jnp.where(source_rock[None], bounced, shifted)
        results.append(jnp.where(blocked[None], current[:, member], pulled))
    return jnp.stack(results, axis=1)


def body_plain(populations, labels, solid, rates):
    scaled = relax_matrix(rates)
    red_part = labels.astype(jnp.float32)[None] * populations
    current = jnp.stack([populations, red_part])
    height = populations.shape[2]
    breadth = populations.shape[3]
    blocked = solid > 0
    grid_shape = current.shape
    solid_pad = padded_2(solid, (("gx", 1), ("gy", 2)), 1) > 0
    for _ in range(ITERS):
        flattened = current.reshape(2, 19, -1)
        moments, red_mass = macroscopic(flattened)
        phase_field = ((2.0 * red_mass - moments[0:1]) / moments[0:1]).reshape(grid_shape[2:])
        padded_phase = padded_2(phase_field, (("gx", 1), ("gy", 2)), 1)
        gradient = gradient_local(padded_phase, height, breadth).reshape(3, -1)
        collided = collide(flattened, moments, red_mass, gradient, scaled).reshape(grid_shape)
        padded = padded_2(collided, (("gx", 3), ("gy", 4)), 1)
        current = stream_local(padded, collided, current, solid_pad, blocked, height, breadth)
    return current


SUB = 8
LANES = 128
HALF = LANES // 2
REACH = 2 * ITERS
SLOT = REACH
INSIDE = 32 - REACH
TURN = 2 * REACH
GROUP = HALF // SLOT
SIDE_COUNT = -(-21 // GROUP)
ROWS = 5 * SUB
FIRST = 2 * SUB
LAST_ROWS = 2 * SUB
HALF_TILE = SUB // 2
FAR_KEPT = REACH - SUB - 1
FAR_PAD = SUB - 2 * FAR_KEPT
FAR_FLAGS = -(-(2 * FAR_PAD + 76 * FAR_KEPT) // SUB) * SUB
PAIRS = [(m, opposite_of(m)) for m in range(1, 19) if m < opposite_of(m)]


def lane_ids(shape):
    return lax.broadcasted_iota(jnp.int32, shape, len(shape) - 1)


def within(shape, *spans):
    ids = lane_ids(shape)
    mask = None
    for first, last in spans:
        for shift in (0, HALF):
            low, high = (first + shift) % LANES, (last + shift) % LANES
            part = (ids >= low) & (ids < high) if low < high else (ids >= low) | (ids < high)
            mask = part if mask is None else mask | part
    return mask


def lane_roll(value, amount):
    return pltpu.roll(value, amount % LANES, axis=value.ndim - 1)


def moved_apart(planes, swap, along):
    if swap:
        planes = planes[::-1]
    return [lane_roll(p, along) for p in planes] if along else planes


def moved_zone(planes, swap, along):
    amount = (HALF if swap else 0) + along
    return [lane_roll(p, amount) for p in planes] if amount else planes


def moved_joined(planes, swap, along):
    first, second, side = planes
    if swap:
        first, second = second, first
    amount = (HALF if swap else 0) + along
    if amount:
        first, second, side = (lane_roll(p, amount) for p in (first, second, side))
    if along:
        ids = lane_ids(first.shape)
        edge = 0 if along > 0 else LANES - 1
        at_first = ids == edge
        at_second = ids == (edge + HALF) % LANES
        first, second, side = (
            jnp.where(at_first, side, first),
            jnp.where(at_second, side, second),
            jnp.where(at_first, first, jnp.where(at_second, second, side)),
        )
    return first, second, side


def tile_reader(ref):
    return lambda member, at: ref[2 * member + at]


def far_reader(ref):
    upper = lax.broadcasted_iota(jnp.int32, (SUB, LANES), 0) < HALF_TILE

    def cells(member, at):
        index = 2 * member + at
        if member >= 19:
            return ref[pl.ds(FAR_FLAGS + SUB * (index - 38), SUB), :]
        first = ref[pl.ds(FAR_PAD + 2 * FAR_KEPT * index, SUB), :]
        last = ref[pl.ds(FAR_PAD + 2 * FAR_KEPT * (index + 1) - SUB, SUB), :]
        return jnp.where(upper, first, last)

    return cells


def gather_kernel(pop_ref, lab_ref, sol_ref, main, far_ref, inner_ref, outer_ref):
    for member in range(19):
        for at in range(2):
            main[2 * member + at] = pop_ref[member, at]
    for at in range(2):
        main[38 + at] = lab_ref[at].astype(jnp.float32)
        main[40 + at] = sol_ref[at].astype(jnp.float32)
    for index in range(38):
        place = FAR_PAD + 2 * FAR_KEPT * index
        kept = pl.ds(SUB - FAR_KEPT, FAR_KEPT)
        far_ref[pl.ds(place, FAR_KEPT), :] = pop_ref[index // 2, index % 2, pl.ds(0, FAR_KEPT), :]
        far_ref[pl.ds(place + FAR_KEPT, FAR_KEPT), :] = pop_ref[index // 2, index % 2, kept, :]
    for index in range(4):
        far_ref[pl.ds(FAR_FLAGS + SUB * index, SUB), :] = main[38 + index]
    even = lax.axis_index("gy") % 2 == 0
    low = lane_ids((SUB, LANES)) < HALF
    left_spans = [(SLOT * k, SLOT * k + REACH) for k in range(GROUP)]
    lefts = [within((SUB, LANES), span) for span in left_spans]
    rights = [within((SUB, LANES), (first - REACH, last - REACH)) for first, last in left_spans]
    deep_left = ~low
    deep_rights = [
        (lane_ids((SUB, LANES)) >= HALF - REACH + SLOT * k)
        & (lane_ids((SUB, LANES)) < LANES - REACH + SLOT * k)
        for k in range(GROUP)
    ]
    for index in range(SIDE_COUNT):
        left_all = right_all = None
        for k in range(min(GROUP, 21 - GROUP * index)):
            member = GROUP * index + k
            shallow = main[2 * member]
            if k:
                shallow = lane_roll(shallow, SLOT * k)
            deep = lane_roll(main[2 * member + 1], HALF + SLOT * k)
            left = jnp.where(deep_left, deep, shallow)
            right = jnp.where(deep_rights[k], deep, shallow)
            left_all = left if k == 0 else jnp.where(lefts[k], left, left_all)
            right_all = right if k == 0 else jnp.where(rights[k], right, right_all)
        inner_ref[index] = jnp.where(even, right_all, left_all)
        outer_ref[index] = jnp.where(even, left_all, right_all)


def weighted_sum(values):
    axis = values[1]
    for q in range(2, 7):
        axis = axis + values[q]
    diag = values[7]
    for q in range(8, 19):
        diag = diag + values[q]
    return 12.0 * values[0] + 2.0 * axis + diag


class Stepper:
    pass


def make_stepper(refs, moved, rates_ref):
    state, after, phase, total, inverse, red, mask, rock = refs
    count = state.shape[1]
    stepper = Stepper()
    norms = np.sum(build_moments() ** 2, axis=1)
    free = [1, 2, 4, 6, 8] + list(range(9, 19))
    rate = {row: rates_ref[k] * float(1.0 / norms[row]) for k, row in enumerate(free)}

    def put_macro(j, rows, density, reds, where=None, sign=None):
        inv = 1.0 / density
        sign = (2.0 * reds - density) * inv if sign is None else sign
        values = ((total, density), (inverse, inv), (red, reds), (phase, sign))
        for ref, value in values:
            if where is None:
                ref[j, rows, :] = value
            else:
                pltpu.store(ref.at[j, rows, :], value, mask=where)

    def make_masks(base):
        for member in range(1, 19):
            a, b, c = (int(v) for v in velocity_table[member])
            planes = moved([rock[j, pl.ds(base - a, SUB), :] for j in range(count)], c % 2 == 1, b)
            for j in range(count):
                mask[member - 1, j, pl.ds(base, SUB), :] = planes[j]

    axis_a9 = rate[9] + 4.0 * rate[10]
    cross_9 = rate[9] - 2.0 * rate[10]
    diag_9 = rate[9] + rate[10]
    axis_a11 = rate[11] + 4.0 * rate[12]
    cross_11 = rate[11] - 2.0 * rate[12]
    diag_11 = rate[11] + rate[12]

    def gradient_planes(base):
        before = [phase[j, pl.ds(base - 1, SUB), :] for j in range(count)]
        here = [phase[j, pl.ds(base, SUB), :] for j in range(count)]
        behind = [phase[j, pl.ds(base + 1, SUB), :] for j in range(count)]
        slope = [p - m for p, m in zip(behind, before)]
        both = [p + m for p, m in zip(behind, before)]
        rim = [2.0 * h + s for h, s in zip(here, both)]
        slope_up, slope_down = moved(slope, False, -1), moved(slope, False, 1)
        slope_deep = moved(slope, True, 0)
        here_up, here_down = moved(here, False, -1), moved(here, False, 1)
        here_deep = moved(here, True, 0)
        rim_y = [r + (d + d) for r, d in zip(rim, here_deep)]
        rim_up, rim_down = moved(rim_y, False, -1), moved(rim_y, False, 1)
        rim_z = [r + (u + d) for r, u, d in zip(rim, here_up, here_down)]
        deeper, shallower = moved(rim_z, True, 0), moved(rim_z, True, 0)
        scale = 1.0 / 12.0
        return [
            (
                scale * (2.0 * slope[j] + (slope_up[j] + slope_down[j]) + (slope_deep[j] + slope_deep[j])),
                scale * (rim_up[j] - rim_down[j]),
                scale * (deeper[j] - shallower[j]),
            )
            for j in range(count)
        ]

    def collide_plane(j, base, grads):
        rows = pl.ds(base, SUB)
        gx, gy, gz = grads
        density, inv, reds = total[j, rows, :], inverse[j, rows, :], red[j, rows, :]
        value = [state[q, j, rows, :] for q in range(19)]
        even = {p: value[p] + value[o] for p, o in PAIRS}
        odd = {p: value[p] - value[o] for p, o in PAIRS}
        ex, ey, ez = 2.0 * even[1], 2.0 * even[3], 2.0 * even[5]
        ox, oy, oz = 2.0 * odd[1], 2.0 * odd[3], 2.0 * odd[5]
        pxy, pxz, pyz = even[7] + even[9], even[11] + even[13], even[15] + even[17]
        rxy, rxz, ryz = even[7] - even[9], even[11] - even[13], even[15] - even[17]
        x_xy, y_xy = odd[7] + odd[9], odd[7] - odd[9]
        x_xz, z_xz = odd[11] + odd[13], odd[11] - odd[13]
        y_yz, z_yz = odd[15] + odd[17], odd[15] - odd[17]
        tx, ty, tz = x_xy + x_xz, y_xy + y_yz, z_xz + z_yz
        jx, jy, jz = ox + tx, oy + ty, oz + tz
        ux, uy, uz = jx * inv, jy * inv, jz * inv
        xx, yy, zz = jx * ux, jy * uy, jz * uz
        square = xx + yy + zz
        sum_axis = ex + ey + ez
        sum_diag = pxy + pxz + pyz
        rest = 12.0 * value[0]
        d_energy = 8.0 * sum_diag - 11.0 * sum_axis - 30.0 * rest + 11.0 * density - 19.0 * square
        d_second = sum_diag - 4.0 * sum_axis + 12.0 * rest - 3.0 * density + 5.5 * square
        flat_x = 1.5 * xx - 0.5 * square
        flat_w = 0.5 * (yy - zz)
        a9 = 3.0 * ex - sum_axis - flat_x
        b9 = sum_diag - 3.0 * pyz - flat_x
        a11 = ey - ez - flat_w
        b11 = pxy - pxz - flat_w
        axis_x = (0.5 * axis_a9) * a9 + (0.5 * cross_9) * b9
        diag_x = cross_9 * a9 + diag_9 * b9
        axis_w = (0.5 * axis_a11) * a11 + (0.5 * cross_11) * b11
        diag_w = cross_11 * a11 + diag_11 * b11
        norm2 = gx * gx + gy * gy + gz * gz
        size = jnp.sqrt(norm2)
        inv_bound = 1.0 / jnp.maximum(size, gradient_floor)
        pull = (0.5 * tension) * size
        push = (0.5 * tension) * inv_bound
        iso_axis = (-5.5 * rate[1]) * d_energy - (2.0 * rate[2]) * d_second + pull
        iso_diag = (8.0 * rate[1]) * d_energy + rate[2] * d_second + pull
        iso_rest = (-2.5 * rate[1]) * d_energy + rate[2] * d_second - pull
        out_even = {
            1: iso_axis + 2.0 * axis_x,
            3: iso_axis - axis_x + axis_w,
            5: iso_axis - axis_x - axis_w,
        }
        dxy = iso_diag + diag_x + diag_w
        dxz = iso_diag + diag_x - diag_w
        dyz = iso_diag - 2.0 * diag_x
        sxy = rate[13] * (rxy - jx * uy)
        syz = rate[14] * (ryz - jy * uz)
        sxz = rate[15] * (rxz - jx * uz)
        out_even.update(
            {7: dxy + sxy, 9: dxy - sxy, 11: dxz + sxz, 13: dxz - sxz, 15: dyz + syz, 17: dyz - syz}
        )
        third = 2.0 / 3.0
        qx = rate[4] * (tx - 4.0 * ox + third * jx)
        qy = rate[6] * (ty - 4.0 * oy + third * jy)
        qz = rate[8] * (tz - 4.0 * oz + third * jz)
        mx = rate[16] * (x_xy - x_xz)
        my = rate[17] * (y_yz - y_xy)
        mz = rate[18] * (z_xz - z_yz)
        fx, fy = qx + mx, qy - my
        hx, hz = qx - mx, qz + mz
        ky, kz = qy + my, qz - mz
        out_odd = {
            1: -2.0 * qx,
            3: -2.0 * qy,
            5: -2.0 * qz,
            7: fx + fy,
            9: fx - fy,
            11: hx + hz,
            13: hx - hz,
            15: ky + kz,
            17: ky - kz,
        }
        along = {
            1: gx,
            3: gy,
            5: gz,
            7: gx + gy,
            9: gx - gy,
            11: gx + gz,
            13: gx - gz,
            15: gy + gz,
            17: gy - gz,
        }
        fraction = reds * inv
        mixing = (recolor_beta / 36.0) * reds * (1.0 - fraction)
        mix_axis = mixing * inv_bound
        mix_diag = mix_axis * float(1.0 / np.sqrt(2.0))
        relaxed = value[0] - iso_rest
        after[0, j, rows, :] = relaxed
        after[19, j, rows, :] = fraction * relaxed
        for p, o in PAIRS:
            steady = out_even[p] - (along[p] * along[p]) * push
            mixed = along[p] * (mix_axis if p < 7 else mix_diag)
            forth = value[p] - (steady + out_odd[p])
            reverse = value[o] - (steady - out_odd[p])
            after[p, j, rows, :] = forth
            after[o, j, rows, :] = reverse
            after[19 + p, j, rows, :] = fraction * forth + mixed
            after[19 + o, j, rows, :] = fraction * reverse - mixed

    def collide_rows(base):
        grads = gradient_planes(base)
        for j in range(count):
            collide_plane(j, base, grads[j])

    def stream_rows(base):
        rows = pl.ds(base, SUB)
        fluid = [rock[j, rows, :] < 0.5 for j in range(count)]
        sums = [[[] for _ in range(count)] for _ in range(2)]
        for q in range(19):
            a, b, c = (int(v) for v in velocity_table[q])
            back_rows = pl.ds(base - a, SUB)
            if q > 0:
                hits = [mask[q - 1, j, rows, :] > 0.5 for j in range(count)]
            for s in range(2):
                planes = [after[19 * s + q, j, back_rows, :] for j in range(count)]
                if q > 0:
                    planes = moved(planes, c % 2 == 1, b)
                    other = 19 * s + opposite_of(q)
                    planes = [
                        jnp.where(hits[j], after[other, j, rows, :], planes[j]) for j in range(count)
                    ]
                for j in range(count):
                    pltpu.store(state.at[19 * s + q, j, rows, :], planes[j], mask=fluid[j])
                    sums[s][j].append(planes[j])
        for j in range(count):
            put_macro(j, rows, weighted_sum(sums[0][j]), weighted_sum(sums[1][j]), fluid[j])

    def fill(values, labels, rocks, rows):
        sums = [[] for _ in range(count)]
        for member in range(19):
            planes = values(member)
            for j in range(count):
                state[member, j, rows, :] = planes[j]
                state[19 + member, j, rows, :] = labels[j] * planes[j]
                sums[j].append(planes[j])
        for j in range(count):
            rock[j, rows, :] = rocks[j]
            density = weighted_sum(sums[j])
            put_macro(j, rows, density, labels[j] * density, sign=2.0 * labels[j] - 1.0)

    def run_early():
        rows_loop(FIRST - REACH + 2, SUB + 2 * REACH - 4, make_masks)
        for iteration in range(ITERS - 1):
            width = REACH - 2 * iteration
            rows_loop(FIRST - width + 1, SUB + 2 * width - 2, collide_rows)
            rows_loop(FIRST - width + 2, SUB + 2 * width - 4, stream_rows)

    stepper.put_macro, stepper.fill, stepper.run_early = put_macro, fill, run_early
    stepper.collide_rows = collide_rows
    return stepper


def rows_loop(start, count, run):
    for index in range(-(-count // SUB)):
        run(start + index * SUB)


def tile_places(spots):
    return [pl.ds(pl.multiple_of(spot * SUB, SUB), SUB) for spot in spots]


def early_kernel(mains, rates_ref, own_ref, rock_ref, zone_ref, *scratch):
    state, rock = scratch[0], scratch[-1]
    stepper = make_stepper(scratch, moved_apart, rates_ref)
    shape = (SUB, LANES)
    ids = lane_ids(shape)
    deep = (ids >= HALF - INSIDE) & (ids < LANES - INSIDE)
    left = within(shape, (TURN, TURN + INSIDE))
    for source, (main, spots) in enumerate(zip(mains, tile_spots(lax.axis_index("gx"), len(mains)))):
        read = tile_reader(main) if source < 3 else far_reader(main)
        cells = [[read(member, 0), read(member, 1)] for member in range(21)]
        for rows in tile_places(spots):
            stepper.fill(lambda member: cells[member], cells[19], cells[20], rows)
        for member in range(21):
            shallow, below = cells[member]
            below = lane_roll(below, HALF)
            right_part = jnp.where(deep, below, shallow)
            left_part = lane_roll(jnp.where(ids < HALF, shallow, below), TURN)
            zone_ref[source * 21 + member] = jnp.where(left, left_part, right_part)
    stepper.run_early()
    for tile in range(LAST_ROWS // SUB):
        rows, here = pl.ds(tile * SUB, SUB), pl.ds(FIRST - 2 + tile * SUB, SUB)
        for q in range(38):
            own_ref[q, 0, rows, :] = state[q, 0, here, :]
            own_ref[q, 1, rows, :] = lane_roll(state[q, 1, here, :], HALF)
        rock_ref[0, rows, :] = rock[0, here, :]
        rock_ref[1, rows, :] = lane_roll(rock[1, here, :], HALF)


def late_kernel(sides, own_ref, rock_ref, zone_ref, rates_ref, out_ref, *scratch):
    zone_scratch, last_scratch = scratch[:8], scratch[8:16]
    out_tile, out_sem = scratch[16:]
    cuts, copies = [6, 12, 18], []
    shape = (SUB, LANES)
    ids = lane_ids(shape)
    sources = zone_ref.shape[0] // 21
    even = lax.axis_index("gy") % 2 == 0
    zone = make_stepper(zone_scratch, moved_zone, rates_ref)
    is_ahead = within(shape, (0, REACH))
    is_behind = within(shape, (REACH, TURN))
    for source, spots in enumerate(tile_spots(lax.axis_index("gx"), sources)):
        planes = []
        for member in range(21):
            index, k = member // GROUP, member % GROUP
            if k == 0:
                inner, outer = sides[source][index], sides[source][SIDE_COUNT + index]
                ahead_pack = jnp.where(even, inner, outer)
                behind_pack = jnp.where(even, outer, inner)
            ahead = lane_roll(ahead_pack, -SLOT * k) if k else ahead_pack
            behind = lane_roll(behind_pack, TURN - SLOT * k)
            own = zone_ref[source * 21 + member]
            planes.append(jnp.where(is_ahead, ahead, jnp.where(is_behind, behind, own)))
        for rows in tile_places(spots):
            zone.fill(lambda member: [planes[member]], [planes[19]], [planes[20]], rows)
    zone.run_early()

    last = make_stepper(last_scratch, moved_joined, rates_ref)
    state, after, rock = last_scratch[0], last_scratch[1], last_scratch[-1]
    lost = 2 * (ITERS - 1)
    from_left = [(ids >= at) & (ids < at + lost) for at in (0, HALF)]
    from_right = [(ids >= at - lost) & (ids < at) for at in (LANES, HALF)]
    right_side = within(shape, (0, 32))
    for tile in range(LAST_ROWS // SUB):
        rows, here = pl.ds(tile * SUB, SUB), pl.ds(FIRST - 2 + tile * SUB, SUB)

        def joined(around, own):
            turned = lane_roll(around, -TURN)
            planes = [
                jnp.where(from_left[j], turned, jnp.where(from_right[j], around, own[j]))
                for j in range(2)
            ]
            return planes + [jnp.where(right_side, around, turned)]

        planes = joined(zone_scratch[-1][0, here, :], [rock_ref[j, rows, :] for j in range(2)])
        for j in range(3):
            rock[j, rows, :] = planes[j]
        sums = [[[] for _ in range(3)] for _ in range(2)]
        for q in range(38):
            own = [own_ref[q, j, rows, :] for j in range(2)]
            planes = joined(zone_scratch[0][q, 0, here, :], own)
            for j in range(3):
                state[q, j, rows, :] = planes[j]
                sums[q // 19][j].append(planes[j])
        for j in range(3):
            last.put_macro(j, rows, weighted_sum(sums[0][j]), weighted_sum(sums[1][j]))
    rows_loop(1, SUB + 2, last.collide_rows)
    rows = pl.ds(2, SUB)
    fluid = [rock[j, rows, :] < 0.5 for j in range(2)]
    for q in range(19):
        a, b, c = (int(v) for v in velocity_table[q])
        back_rows = pl.ds(2 - a, SUB)
        hits = moved_joined([rock[j, back_rows, :] for j in range(3)], c % 2 == 1, b)
        for s in range(2):
            planes = [after[19 * s + q, j, back_rows, :] for j in range(3)]
            planes = moved_joined(planes, c % 2 == 1, b)
            for j in range(2):
                value = planes[j]
                if q > 0:
                    bounced = after[19 * s + opposite_of(q), j, rows, :]
                    value = jnp.where(hits[j] > 0.5, bounced, value)
                value = jnp.where(fluid[j], value, state[19 * s + q, j, rows, :])
                out_tile[s, q, j] = lane_roll(value, HALF) if j else value
        if q in cuts:
            number = cuts.index(q)
            first = cuts[number - 1] + 1 if number else 0
            for s in range(2):
                part = (s, pl.ds(first, q + 1 - first))
                copy = pltpu.make_async_copy(
                    out_tile.at[part], out_ref.at[part], out_sem.at[s, number]
                )
                copy.start()
                copies.append(copy)
    for copy in copies:
        copy.wait()


def next_pairs(count):
    return [i ^ 1 for i in range(count)]


def other_pairs(count):
    return [(i + 1 if i % 2 else i - 1) % count for i in range(count)]


def far_pairs(count):
    first = [i + 2 if i % 4 < 2 else i - 2 for i in range(count)]
    second = [(i - 2 if i % 4 < 2 else i + 2) % count for i in range(count)]
    return [first] if first == second else [first, second]


def tile_spots(index, count):
    odd = index % 2
    late = (index // 2) % 2
    near = [(2,), (3 - 2 * odd,), (1 + 2 * odd,)]
    if count == 4:
        return near + [(0, 4)]
    return near + [(4 - 4 * late,), (4 * late,)]


def swapped(value, axis, partners):
    return lax.ppermute(value, axis, list(enumerate(partners)))


def vmem_call(kernel, out_shapes, args, rates=None, scratch=(), out_specs=None):
    vmem = pl.BlockSpec(memory_space=pltpu.VMEM)
    specs = [vmem] * len(args)
    args = [pltpu.with_memory_space_constraint(arg, pltpu.VMEM) for arg in args]
    if rates is not None:
        specs.append(pl.BlockSpec(memory_space=pltpu.SMEM))
        args.append(rates)
    kept = {} if out_specs is None else {"out_specs": out_specs}
    return pl.pallas_call(
        kernel, out_shape=out_shapes, in_specs=specs, scratch_shapes=scratch, **kept
    )(*args)


def scratch_planes(count, rows):
    plane = pltpu.VMEM((count, rows, LANES), jnp.float32)
    full = pltpu.VMEM((38, count, rows, LANES), jnp.float32)
    masks = pltpu.VMEM((18, count, rows, LANES), jnp.float32)
    return [full, full, plane, plane, plane, plane, masks, plane]


def body_deep(populations, labels, solid, rates):
    high, wide = lax.axis_size("gx"), lax.axis_size("gy")
    patterns = [next_pairs(high), other_pairs(high)] + far_pairs(high)
    number = 1 + len(patterns)

    def planes(*shape):
        return pltpu.VMEM(shape + (LANES,), jnp.float32)

    def early(*refs):
        early_kernel(refs[:number], *refs[number:])

    def late(*refs):
        late_kernel(refs[:number], *refs[number:])

    border = planes(SIDE_COUNT, SUB)
    shapes = (planes(42, SUB), planes(FAR_FLAGS + 4 * SUB), border, border)
    main, far, inner, outer = pl.pallas_call(gather_kernel, out_shape=shapes)(
        populations, labels, solid
    )
    mains = [main] + [
        swapped(main if k < 2 else far, "gx", partners) for k, partners in enumerate(patterns)
    ]
    outer = swapped(outer, "gy", other_pairs(wide))
    inner = swapped(inner, "gy", next_pairs(wide))
    side = jnp.concatenate([inner, outer], axis=0)
    sides = [side] + [swapped(side, "gx", partners) for partners in patterns]
    kept = (planes(38, 2, LAST_ROWS), planes(2, LAST_ROWS), planes(number * 21, SUB))
    own, rock, zone = vmem_call(early, kept, mains, rates, scratch_planes(2, ROWS))
    return vmem_call(
        late,
        jax.ShapeDtypeStruct((2,) + populations.shape, jnp.float32),
        sides + [own, rock, zone],
        rates,
        scratch_planes(1, ROWS)
        + scratch_planes(3, LAST_ROWS + SUB)
        + [planes(2, 19, 2, SUB), pltpu.SemaphoreType.DMA((2, 3))],
        pl.BlockSpec(memory_space=pl.ANY),
    )


def body(populations, labels, solid, rates):
    depth, height, breadth = populations.shape[1:]
    fits = (depth, height, breadth) == (2, SUB, LANES)
    fits = fits and lax.axis_size("gx") % 4 == 0 and lax.axis_size("gy") % 2 == 0
    if fits and SUB < REACH < 2 * SUB and HALF == 2 * (REACH + INSIDE):
        return body_deep(populations, labels, solid, rates)
    return body_plain(populations, labels, solid, rates)


def solution(mesh):
    return jax.shard_map(
        body,
        mesh=mesh,
        in_specs=(P(None, None, "gx", "gy"), P(None, "gx", "gy"), P(None, "gx", "gy"), P()),
        out_specs=P(None, None, None, "gx", "gy"),
        check_vma=False,
    )
```
